32 devices in a mesh: groups: 2 (over y), seq: 16 (over z, x, core).
Axes of the slice: x: 2, y: 2, z: 4, core: 2. Of those that a mesh axis runs over, the one named last changes fastest.
Arguments:
- bases: int32 [8192], P(('groups', 'seq')), parts along dimension 0, may hold values from 0 to 3
- base_table: bfloat16 [4, 768], replicated, may hold values from -4 to 4
- first_kernel: bfloat16 [768, 864], P('seq'), may hold values from -0.21875 to 0.21875
- second_kernel: bfloat16 [768, 864], P('seq'), may hold values from -0.21875 to 0.21875
- cotangent: bfloat16 [8192, 768], P(('groups', 'seq')), parts along dimension 0, may hold values from -0.125 to 0.125
Outputs:
- combined: bfloat16 [8192, 768], P(('groups', 'seq')), parts along dimension 0
- first_grad: float32 [1536, 864], P(('groups', 'seq')), parts along dimension 0
- second_grad: float32 [1536, 864], P(('groups', 'seq')), parts along dimension 0
The draws below stay inside these ranges and needn't reach their ends.
There are 2 independent parts, one for each index of `groups`. The reference program is written for one: setup_inputs(seed, part) draws one part's arguments, and reference() takes and returns one part's arrays. A program takes and returns all parts, laid end to end along the dimension named above; an argument that names none is the same for every part. Nothing has to cross between parts.
Inputs may be any that keep to these rules, and one draw needn't show every extreme that they name: `bases`: base codes; the complement of code b is 3 - b.
All inputs are finite; a program needn't handle non-finite values.
Results may differ from the reference program's by a relative error of at most 0.0044.
Values may be sent and summed in bfloat16 or wider, within the bound.
A program may use at most 128 MiB of HBM per device.

```python
import math
import jax
import jax.numpy as jnp
from jax import lax

D = 768
GROUPS = 8
TAPS = 9
CG = 96
LENGTH = 4096


def with_ends(array, key, low, largest):
    index_at = [jax.random.randint(jax.random.fold_in(key, axis), (), 0, length) for axis, length in enumerate(array.shape)]
    longest = array.shape.index(max(array.shape))
    neighbour = index_at[:longest] + [(index_at[longest] + 1) % array.shape[longest]] + index_at[longest + 1:]
    return array.at[tuple(index_at)].set(low).at[tuple(neighbour)].set(largest)


def strengthened(drawn, rng, source, target, shards_of, factor):
    owner, partner = [(jnp.arange(drawn.shape[position]) // (drawn.shape[position] // shards_of)).reshape([-1 if axis == position else 1 for axis in range(drawn.ndim)]) for position in (source, target)]
    chosen = jax.random.permutation(rng, shards_of)[partner]
    strong = (owner == chosen) | (owner == (partner + shards_of // 2) % shards_of)
    return jnp.where(strong, factor * drawn, drawn)


def block_scale(rng, shape, cuts, least, top_value):
    gain, own = 1.0, jax.random.fold_in(rng, 6)
    for axis_at, blocks in cuts:
        draws = jnp.exp(jax.random.uniform(jax.random.fold_in(own, axis_at), (blocks,), jnp.float32, least / len(cuts), top_value / len(cuts)))
        gain = gain * jnp.repeat(draws, shape[axis_at] // blocks).reshape([-1 if axis == axis_at else 1 for axis in range(len(shape))])
    return gain


def scatter_about(key, shape, scale, bound, cuts=(), kind=jnp.bfloat16):
    array = scale * jax.random.normal(key, shape, jnp.float32)
    if cuts:
        array = array * block_scale(key, shape, cuts, -0.22, 0.18)
    return jnp.clip(array, -bound, bound).astype(kind)


def bell_draw_with(key, shape, spread, reach, split, heavy, kind=jnp.bfloat16):
    drawn = spread * jax.random.normal(key, shape, jnp.float32)
    if split:
        drawn = drawn * block_scale(key, shape, split, -0.22, 0.18)
    return jnp.clip(strengthened(drawn, jax.random.fold_in(key, 3), *heavy), -reach, reach).astype(kind)


def setup_inputs(seed: int = 0, part: int = 0) -> dict:
    splits = jax.random.split(jax.random.key(seed), 6)
    part_splits = jax.random.split(jax.random.fold_in(splits[5], part), 6)
    return {
        "bases": with_ends(jax.random.randint(part_splits[0], (LENGTH,), 0, 4), jax.random.fold_in(part_splits[0], 1), 0, 3).astype(jnp.int32),
        "base_table": scatter_about(splits[1], (4, D), 1.0, 4.0),
        "first_kernel": scatter_about(splits[2], (D, TAPS * CG), (TAPS * CG) ** -0.5, 0.21875, ((0, 16),)),
        "second_kernel": scatter_about(splits[3], (D, TAPS * CG), (TAPS * CG) ** -0.5, 0.21875, ((0, 16),)),
        "cotangent": bell_draw_with(part_splits[4], (LENGTH, D), LENGTH ** -0.5, 0.125, ((0, 16),), (0, 1, 16, 2.0)),
    }


def gelu_exact(values):
    return jax.nn.gelu(values, approximate=False)

def to_taps(kernel):
    return jnp.transpose(kernel.reshape(GROUPS, CG, TAPS, CG), (2, 0, 1, 3))

def from_taps(taps):
    return jnp.transpose(taps, (1, 2, 0, 3)).reshape(D, TAPS * CG)

def adjoint(taps):
    return jnp.swapaxes(taps[::-1], 2, 3)

def block_size():
    return math.gcd(LENGTH, 4096)

def convolve(values, taps):
    half_taps = TAPS // 2
    block_rows = block_size()
    padded = jnp.pad(values, ((half_taps, half_taps), (0, 0))).reshape(-1, GROUPS, CG)
    taps_wide = taps.astype(jnp.float32)

    def one_block(offset):
        window = lax.dynamic_slice_in_dim(padded, offset, block_rows + 2 * half_taps, 0).astype(jnp.float32)
        summed = jnp.zeros((block_rows, GROUPS, CG), jnp.float32)
        for tap_index in range(TAPS):
            summed = summed + jnp.einsum('pgc,goc->pgo', window[tap_index:tap_index + block_rows], taps_wide[tap_index])
        return summed
    offsets = jnp.arange(LENGTH // block_rows, dtype=jnp.int32) * block_rows
    return lax.map(one_block, offsets).reshape(LENGTH, D)

def correlate(grad_rows, values):
    half_taps = TAPS // 2
    block_rows = block_size()
    padded = jnp.pad(values, ((half_taps, half_taps), (0, 0))).reshape(-1, GROUPS, CG)
    grad_groups = grad_rows.reshape(-1, GROUPS, CG)

    def accumulate(summed, offset):
        window = lax.dynamic_slice_in_dim(padded, offset, block_rows + 2 * half_taps, 0).astype(jnp.float32)
        grad_part = lax.dynamic_slice_in_dim(grad_groups, offset, block_rows, 0).astype(jnp.float32)
        terms = jnp.stack([jnp.einsum('pgo,pgc->goc', grad_part, window[tap_index:tap_index + block_rows]) for tap_index in range(TAPS)])
        return (summed + terms, None)
    offsets = jnp.arange(LENGTH // block_rows, dtype=jnp.int32) * block_rows
    summed, _ = lax.scan(accumulate, jnp.zeros((TAPS, GROUPS, CG, CG), jnp.float32), offsets)
    return summed

def strand_pass(inputs, first_taps, second_taps, grad_out):
    pre_act = convolve(inputs, first_taps)
    hidden = gelu_exact(pre_act).astype(jnp.bfloat16)
    strand_out = inputs.astype(jnp.float32) + convolve(hidden, second_taps)
    hidden_grad = convolve(grad_out, adjoint(second_taps))
    _, pullback = jax.vjp(gelu_exact, pre_act)
    pre_grad = pullback(hidden_grad)[0].astype(jnp.bfloat16)
    return (strand_out, correlate(pre_grad, inputs), correlate(grad_out, hidden))

def reference(bases, base_table, first_kernel, second_kernel, cotangent):
    first_taps = to_taps(first_kernel)
    second_taps = to_taps(second_kernel)
    forward_in = base_table[bases]
    reverse_in = base_table[3 - bases[::-1]]
    out_forward, first_f, second_f = strand_pass(forward_in, first_taps, second_taps, cotangent)
    out_reverse, first_r, second_r = strand_pass(reverse_in, first_taps, second_taps, cotangent[::-1])
    rounded = lax.optimization_barrier(out_reverse.astype(jnp.bfloat16))
    combined = (out_forward + rounded.astype(jnp.float32)[::-1]).astype(jnp.bfloat16)
    return (combined, from_taps(first_f + first_r), from_taps(second_f + second_r))
```

```python
import functools
import math

import jax
import jax.numpy as jnp
from jax import lax
from jax.experimental import pallas as pl
from jax.experimental.pallas import tpu as pltpu
from jax.sharding import PartitionSpec as P

GROUPS = 8
TAPS = 9
HALF = TAPS // 2
SPAN = TAPS + 1
LANES = 128
MESH = pl.DeviceIdType.MESH
F32 = jnp.float32
BF16 = jnp.bfloat16


def lane_contract(left, right):
    return lax.dot_general(left, right, (((1,), (1,)), ((), ())), preferred_element_type=F32)


def dot(left, right):
    return jnp.dot(left, right, preferred_element_type=F32)


def iota(shape, axis):
    return lax.broadcasted_iota(jnp.int32, shape, axis)


def split_halves(values):
    high = values.astype(BF16).astype(F32)
    return jnp.where((iota(values.shape, 1) & 7) < 4, high, values - high).astype(BF16)


def group_of(place):
    return place // 2 + (GROUPS // 2) * (place % 2)


def place_of(group):
    return (group % (GROUPS // 2)) * 2 + group // (GROUPS // 2)


def gelu_and_slope(pre):
    z = jnp.abs(pre) * math.sqrt(0.5)
    t = pl.reciprocal(1.0 + 0.3275911 * z)
    e = jnp.exp(-0.5 * pre * pre)
    series = 1.061405429
    for c in (-1.453152027, 1.421413741, -0.284496736, 0.254829592):
        series = series * t + c
    tail = (0.5 * series) * (t * e)
    cdf = jnp.where(pre < 0, tail, 1.0 - tail)
    return pre * cdf, cdf + pre * (e * (1.0 / math.sqrt(2.0 * math.pi)))


def block_kernel(
    count, members, gathered,
    bases_hbm, table_hbm, first_hbm, second_hbm, cot_hbm,
    comb_out, first_out, second_out,
    bases_ref, table_ref, first_ref, second_ref, cot_ref,
    diag_ref, skip_ref, codes_ref, cot_perm, cot_t, edges,
    codes_in, codes_left, codes_right, mix_send, mix_in, second_in,
    cot_in, cot_left, cot_right, comb_send, comb_in, s_send, s_in, t_send, t_in,
    onehot, hid, slope, unf, cot_unf, r_acc, lhs_out, lhs_grad,
    send_sems, recv_sems, load_sems,
):
    me = lax.axis_index("seq")
    chunk_of = me // GROUPS
    place = me % GROUPS
    group = group_of(place)
    chunks = count // GROUPS
    band = cot_ref.shape[0]
    cg = cot_in.shape[0]
    pair = 2 * cg
    taps = TAPS * cg
    span = SPAN * cg
    half = band // 2
    q = half * GROUPS
    width = q + LANES
    channels = GROUPS * cg
    rows = cg if gathered else cg // members
    owner = me // members
    member = me % members
    started = []

    def push(src, dst, kind, recv, target, here=None):
        remote = pltpu.make_async_remote_copy(
            src_ref=src, dst_ref=dst, send_sem=send_sems.at[kind], recv_sem=recv_sems.at[recv],
            device_id={"seq": target}, device_id_type=MESH,
        )
        away = target != me
        if here is not None:
            away = here & away
            local = here & (target == me)
        else:
            local = target == me

        @pl.when(away)
        def _():
            remote.start()

        @pl.when(local)
        def _():
            pltpu.make_async_copy(src, dst, recv_sems.at[recv]).start()

        started.append((remote, away))

    def arrived(ref, recv):
        pltpu.make_async_copy(ref, ref, recv_sems.at[recv]).wait()

    def push_chunk(src_of, dst, kind, recv):
        for k in range(GROUPS):
            to = (place + k + 1) % GROUPS
            push(src_of(to), dst, kind, recv, chunk_of * GROUPS + to)

    def push_edges(src_of, left_dst, right_dst, kind, recv_left, recv_right):
        for low, dst, recv, here, there in (
            (True, right_dst, recv_right, (place == 0) & (chunk_of > 0), chunk_of - 1),
            (False, left_dst, recv_left, (place == GROUPS - 1) & (chunk_of < chunks - 1), chunk_of + 1),
        ):
            for to in range(GROUPS):
                push(src_of(to, low), dst, kind, recv, there * GROUPS + to, here)

    def edges_arrived(left, right, recv_left, recv_right):
        @pl.when(chunk_of > 0)
        def _():
            arrived(left, recv_left)

        @pl.when(chunk_of < chunks - 1)
        def _():
            arrived(right, recv_right)

    barrier = pltpu.get_barrier_semaphore()
    for k in range(1, count):
        pl.semaphore_signal(barrier, inc=1, device_id={"seq": (me + k) % count}, device_id_type=MESH)

    loads = [
        pltpu.make_async_copy(src, dst, load_sems.at[k])
        for k, (src, dst) in enumerate(
            (
                (bases_hbm, bases_ref), (table_hbm, table_ref), (first_hbm, first_ref),
                (cot_hbm, cot_ref), (second_hbm, second_ref),
            )
        )
    ]
    for load in loads:
        load.start()

    spread = (iota((band, band), 1) == 2 * (iota((band, band), 0) % half) + iota((band, band), 0) // half)
    spread = spread.astype(F32).astype(BF16)
    loads[0].wait()
    bases = jnp.broadcast_to(bases_ref[...], (8, band)).astype(F32).astype(BF16)
    codes = lane_contract(bases, spread)
    codes_ref[0:8] = codes[:, :half]
    codes_ref[8:16] = codes[:, half:]

    loads[1].wait()
    table = table_ref[...].astype(F32)
    code = iota((8, channels), 0)
    wide = jnp.zeros((8, channels), F32)
    turned = jnp.zeros((8, channels), F32)
    for c in range(4):
        wide = jnp.where(code % 4 == c, table[c : c + 1], wide)
        turned = jnp.where(code == 7 - c, table[c : c + 1], turned)
    lane = iota((8, channels), 1)
    whose = group if gathered else owner
    strand = jnp.where(lane < cg, pltpu.roll(wide, (channels - whose * cg) % channels, 1), 0.0)
    strand = jnp.concatenate([strand, jnp.zeros((8, LANES), F32)], axis=1)
    diag_ref[...] = jnp.concatenate([pltpu.roll(strand, cg * t, 1) for t in range(TAPS)], axis=0)[:, :taps].astype(BF16)
    own = pltpu.roll(jnp.where(code < 4, wide, turned), (channels - group * cg) % channels, 1)[:, :cg]
    eye = (iota((band, band), 0) == iota((band, band), 1)).astype(F32).astype(BF16)
    skip_ref[...] = lane_contract(
        eye[:cg, :cg],
        jnp.concatenate([own, jnp.zeros((8, cg), F32)], axis=0).astype(BF16),
    ).astype(BF16)
    loads[2].wait()
    mix = split_halves(lane_contract(first_ref[...], diag_ref[...]))
    if gathered:
        mix_in[0, :, : 8 * TAPS] = mix
    else:
        mix_send[:, : 8 * TAPS] = mix

    loads[3].wait()
    for j in range(channels // band):
        cot_perm[:, band * j : band * (j + 1)] = dot(
            spread, cot_ref[:, band * j : band * (j + 1)]
        ).astype(BF16)
    for j in range(channels // band):
        cot_t[band * j : band * (j + 1)] = lane_contract(
            eye, cot_perm[:, band * j : band * (j + 1)]
        ).astype(BF16)
    for to in range(GROUPS):
        g = group_of(to)
        for b in range(2):
            edges[0, to, b] = cot_perm[half * b : half * b + 16, cg * g : cg * (g + 1)]
            edges[1, to, b] = cot_perm[half * (b + 1) - 16 : half * (b + 1), cg * g : cg * (g + 1)]

    loads[4].wait()
    pl.semaphore_wait(barrier, count - 1)

    here = pl.ds(pl.multiple_of(place * half, LANES), half)
    push_chunk(lambda to: codes_ref, codes_in.at[:, here], 0, 0)
    push_edges(lambda to, low: codes_ref, codes_left, codes_right, 1, 1, 2)
    if not gathered:
        for c in range(chunks):
            push(mix_send, mix_in.at[member], 2, 3, c * GROUPS + place_of(owner))
        for c in range(chunks):
            push(second_ref, second_in.at[member], 3, 4, c * GROUPS + place_of(owner))
    here = pl.ds(pl.multiple_of(place * band, LANES), band)
    push_chunk(
        lambda to: cot_t.at[pl.ds(pl.multiple_of(group_of(to) * cg, 16), cg)], cot_in.at[:, here], 4, 5
    )
    push_edges(lambda to, low: edges.at[0 if low else 1, to], cot_left, cot_right, 5, 6, 7)

    has_right = (chunk_of < chunks - 1).astype(jnp.int32)
    has_left = (chunk_of > 0).astype(jnp.int32)

    def edge_mask(height):
        lane = iota((height, LANES), 1)
        return lane < LANES // 2, jnp.where(lane < LANES // 2, has_right, has_left) > 0

    unf[span + 16 : span + 64, :] = jnp.zeros((48, q), BF16)
    for a in range(2):
        for s in range(2):
            hid[a, LANES * s + cg : LANES * (s + 1), :] = jnp.zeros((LANES - cg, width), BF16)
    arrived(codes_in, 0)
    edges_arrived(codes_left, codes_right, 1, 2)
    on_right, real = edge_mask(16)
    edge = jnp.where(real, jnp.where(on_right, codes_right[...], codes_left[...]), 4.0)
    codes = jnp.concatenate([codes_in[...], edge], axis=1)
    want = (iota((8, width), 0) & 3).astype(F32)
    moved = {}
    for b in range(2):
        for s in range(-2, 3):
            line = codes[8 * b : 8 * (b + 1)]
            moved[s, b] = line if s == 0 else pltpu.roll(line, (-s) % width, 1)
    for strand in range(2):
        blocks = []
        for j in range(SPAN):
            value = moved[j // 2 - 2, j % 2] if strand == 0 else 3.0 - moved[2 - j // 2, 1 - j % 2]
            blocks.append(jnp.where(value == want, 1.0, 0.0))
        onehot[strand] = jnp.concatenate(blocks, axis=0).astype(BF16)
    unf[span : span + 16, :] = onehot[0, 8 * HALF : 8 * HALF + 16, :q]

    if not gathered:
        arrived(mix_in, 3)
    mix = mix_in[...].reshape(cg, LANES).astype(F32)
    mix = jnp.where(iota((cg, LANES), 1) < 8 * TAPS, mix, 0.0)
    mix = jnp.concatenate([mix, pltpu.roll(mix, 8, 1)], axis=0)[:, : 8 * SPAN].astype(BF16)

    def store_hidden(strand, cols, hidden):
        for k in range(2):
            hid[k if strand == 0 else 1 - k, LANES * strand : LANES * strand + cg, cols] = hidden[cg * k : cg * (k + 1)]

    @pl.loop(0, q // 256)
    def _(i):
        cols = pl.ds(pl.multiple_of(i * 256, 256), 256)
        for strand in range(2):
            hidden, grad = gelu_and_slope(dot(mix, onehot[strand, :, cols]))
            store_hidden(strand, cols, hidden.astype(BF16))
            slope[pair * strand : pair * (strand + 1), cols] = grad

    _, real = edge_mask(pair)
    for strand in range(2):
        hidden, _ = gelu_and_slope(dot(mix, onehot[strand, :, q:]))
        store_hidden(strand, slice(q, width), jnp.where(real, hidden, 0.0).astype(BF16))

    for b in range(2):
        for strand in range(2):
            line = hid[b, LANES * strand : LANES * strand + cg, :]
            for s in range(-2, 3):
                j = 2 * (s + 2) + b if strand == 0 else 2 * (2 - s) + 1 - b
                top = strand * (span + 64) + cg * j
                unf[top : top + cg, :] = (line if s == 0 else pltpu.roll(line, (-s) % width, 1))[:, :q]

    if gathered:
        second = second_ref[...]
    else:
        arrived(second_in, 4)
        second = second_in[...].reshape(cg, taps)
    low = jnp.concatenate([second, jnp.zeros((cg, cg), BF16)], axis=1)
    high = jnp.concatenate([jnp.zeros((cg, cg), BF16), second], axis=1)
    blank = jnp.zeros((cg, 48), BF16)
    own = skip_ref[...]
    lhs_out[0:cg] = jnp.concatenate([low, own, blank, high], axis=1)
    lhs_out[cg:] = jnp.concatenate(
        [high, pltpu.roll(jnp.concatenate([own, jnp.zeros((cg, LANES - 16), BF16)], axis=1).astype(F32), 8, 1)[:, :16].astype(BF16), blank, low],
        axis=1,
    )

    @pl.loop(0, q // 256, unroll=True)
    def _(i):
        cols = pl.ds(pl.multiple_of(i * 256, 256), 256)
        out = dot(lhs_out[...], unf[:, cols]).astype(BF16)
        for k in range(256 // half):
            at = pl.ds(pl.multiple_of((i * (256 // half) + k) * band, LANES), band)
            comb_send[:, at] = jnp.concatenate(
                [out[:cg, half * k : half * (k + 1)], out[cg:, half * k : half * (k + 1)]], axis=1
            )
            target = chunk_of * GROUPS + i * (256 // half) + k
            remote = pltpu.make_async_remote_copy(
                src_ref=comb_send.at[:, at], dst_ref=comb_in.at[group], send_sem=send_sems.at[6],
                recv_sem=recv_sems.at[8], device_id={"seq": target}, device_id_type=MESH,
            )

            @pl.when(target != me)
            def _():
                remote.start()

            @pl.when(target == me)
            def _():
                pltpu.make_async_copy(comb_send.at[:, at], comb_in.at[group], recv_sems.at[8]).start()

    for k in range(GROUPS):
        target = chunk_of * GROUPS + k
        remote = pltpu.make_async_remote_copy(
            src_ref=comb_send.at[:, pl.ds(k * band, band)], dst_ref=comb_in.at[group], send_sem=send_sems.at[6],
            recv_sem=recv_sems.at[8], device_id={"seq": target}, device_id_type=MESH,
        )
        started.append((remote, target != me))

    stack = []
    for t in range(SPAN):
        lowered = second[:, cg * (8 - t) : cg * (9 - t)] if t < TAPS else jnp.zeros((cg, cg), BF16)
        raised = second[:, cg * (9 - t) : cg * (10 - t)] if t > 0 else jnp.zeros((cg, cg), BF16)
        before = second[:, cg * (t - 1) : cg * t] if t > 0 else jnp.zeros((cg, cg), BF16)
        after = second[:, cg * t : cg * (t + 1)] if t < TAPS else jnp.zeros((cg, cg), BF16)
        stack.append(jnp.concatenate([lowered, raised, before, after], axis=1))
    stack = jnp.concatenate(stack, axis=0)
    for strand in range(2):
        lhs_grad[pair * strand : pair * (strand + 1)] = lane_contract(
            eye[:pair, :pair], stack[:, pair * strand : pair * (strand + 1)]
        ).astype(BF16)

    arrived(cot_in, 5)
    edges_arrived(cot_left, cot_right, 6, 7)
    for b in range(2):
        edge = lane_contract(
            eye[:cg, :cg],
            jnp.concatenate(
                [
                    jnp.where(has_right > 0, cot_right[b].astype(F32), 0.0),
                    jnp.zeros((LANES - 32, cg), F32),
                    jnp.where(has_left > 0, cot_left[b].astype(F32), 0.0),
                ],
                axis=0,
            ).astype(BF16),
        ).astype(BF16)
        line = jnp.concatenate(
            [cot_in[:, band * k + half * b : band * k + half * (b + 1)] for k in range(GROUPS)] + [edge], axis=1
        )
        for s in range(-2, 3):
            top = cg * (2 * (s + 2) + b)
            cot_unf[top : top + cg, :] = (line if s == 0 else pltpu.roll(line, (-s) % width, 1))[:, :q]

    forward = cot_unf[2 * pair : 3 * pair, :]
    reverse = jnp.concatenate([forward[cg:], forward[:cg]], axis=0)
    for n in range(0, span, 256):
        size = min(256, span - n)
        r_acc[:, n : n + size] = lane_contract(forward, unf[n : n + size, :]) + lane_contract(
            reverse, unf[span + 64 + n : span + 64 + n + size, :]
        )
    total = r_acc[0:cg, :taps] + pltpu.roll(r_acc[cg:, :], r_acc.shape[1] - cg, 1)[:, :taps]
    if gathered:
        s_in[0, :, :taps] = total.astype(BF16)
    else:
        for k in range(members):
            s_send[k, :, :taps] = total[rows * k : rows * (k + 1)].astype(BF16)
        for k in range(members):
            push(s_send.at[k], s_in.at[chunk_of], 7, 9, group * members + k)

    def backward(i, total):
        cols = pl.ds(pl.multiple_of(i * 256, 256), 256)
        grad = dot(lhs_grad[...], cot_unf[:, cols])
        pre_grad = (grad * slope[:, cols]).astype(BF16)
        return (
            total
            + lane_contract(pre_grad[:pair], onehot[0, :, cols])
            + lane_contract(pre_grad[pair:], onehot[1, :, cols])
        )

    terms = lax.fori_loop(0, q // 256, backward, jnp.zeros((pair, 8 * SPAN), F32), unroll=True)
    shifted = jnp.concatenate([terms[cg:], jnp.zeros((cg, LANES - 8 * SPAN), F32)], axis=1)
    terms = terms[:cg, : 8 * TAPS] + pltpu.roll(shifted, LANES - 8, 1)[:, : 8 * TAPS]
    if gathered:
        t_in[0, :, : 8 * TAPS] = terms
    else:
        for k in range(members):
            t_send[k, :, : 8 * TAPS] = terms[rows * k : rows * (k + 1)]
        for k in range(members):
            push(t_send.at[k], t_in.at[chunk_of], 8, 10, group * members + k)

    arrived(comb_in, 8)
    for j in range(channels // band):
        part = comb_in[...].reshape(channels, band)[band * j : band * (j + 1)]
        gather = (iota((band, band), 1) == (iota((band, band), 0) % 2) * half + iota((band, band), 0) // 2)
        comb_out[:, band * j : band * (j + 1)] = lane_contract(gather.astype(F32).astype(BF16), part).astype(BF16)
    if not gathered:
        arrived(s_in, 9)
    second_out[...] = jnp.sum(s_in[:, :, :taps].astype(F32), axis=0)
    if not gathered:
        arrived(t_in, 10)
    first_out[...] = dot(split_halves(jnp.sum(t_in[:, :, : 8 * TAPS], axis=0)), diag_ref[...])

    for remote, away in started:
        @pl.when(away)
        def _():
            remote.wait_send()


def finish_kernel(*refs):
    sems = refs[6]
    copies = [pltpu.make_async_copy(refs[k], refs[3 + k], sems.at[k]) for k in range(3)]
    for copy in copies:
        copy.start()
    for copy in copies:
        copy.wait()


def per_device(bases, base_table, first_kernel, second_kernel, cotangent):
    band, channels = cotangent.shape
    cg = channels // GROUPS
    count = lax.axis_size("seq")
    members = count // GROUPS
    rows = first_kernel.shape[0]
    gathered = rows % 16 != 0
    half = band // 2
    q = half * GROUPS
    width = q + LANES
    pair = 2 * cg
    taps = TAPS * cg
    span = SPAN * cg
    deep = 2 * span + 64

    lot = 1 if gathered else members
    if gathered:
        group = group_of(lax.axis_index("seq") % GROUPS)
        first_kernel, second_kernel = (
            lax.dynamic_slice_in_dim(lax.all_gather(k, "seq", axis=0, tiled=True), group * cg, cg, 0)
            for k in (first_kernel, second_kernel)
        )
        rows = cg

    vmem = pltpu.VMEM
    outs = pl.pallas_call(
        functools.partial(block_kernel, count, members, gathered),
        out_shape=(
            vmem((band, channels), BF16),
            vmem((rows, taps), F32),
            vmem((rows, taps), F32),
        ),
        in_specs=[pl.BlockSpec(memory_space=pl.ANY)] * 5,
        out_specs=[pl.BlockSpec(memory_space=vmem)] * 3,
        scratch_shapes=[
            vmem((1, band), jnp.int32),
            vmem(base_table.shape, BF16),
            vmem(first_kernel.shape, BF16),
            vmem(second_kernel.shape, BF16),
            vmem((band, channels), BF16),
            vmem((8 * TAPS, taps), BF16),
            vmem((cg, 16), BF16),
            vmem((16, half), F32),
            vmem((band, channels), BF16),
            vmem((channels, band), BF16),
            vmem((2, GROUPS, 2, 16, cg), BF16),
            vmem((16, q), F32),
            vmem((16, LANES), F32),
            vmem((16, LANES), F32),
            vmem((rows, LANES), BF16),
            vmem((lot, rows, LANES), BF16),
            vmem((lot, rows, taps), BF16),
            vmem((cg, 2 * q), BF16),
            vmem((2, 16, cg), BF16),
            vmem((2, 16, cg), BF16),
            vmem((cg, 2 * q), BF16),
            vmem((GROUPS, cg, band), BF16),
            vmem((lot, rows, taps), BF16),
            vmem((lot, rows, taps), BF16),
            vmem((lot, rows, LANES), F32),
            vmem((lot, rows, LANES), F32),
            vmem((2, 8 * SPAN, width), BF16),
            vmem((2, 2 * LANES, width), BF16),
            vmem((2 * pair, q), F32),
            vmem((deep, q), BF16),
            vmem((span, q), BF16),
            vmem((pair, span + 64), F32),
            vmem((pair, deep), BF16),
            vmem((2 * pair, span), BF16),
            pltpu.SemaphoreType.DMA((9,)),
            pltpu.SemaphoreType.DMA((11,)),
            pltpu.SemaphoreType.DMA((5,)),
        ],
        compiler_params=pltpu.CompilerParams(
            collective_id=0, has_side_effects=True, vmem_limit_bytes=56 * 1024 * 1024
        ),
    )(bases.reshape(1, band), base_table, first_kernel, second_kernel, cotangent)

    outs = pl.pallas_call(
        finish_kernel,
        out_shape=tuple(jax.ShapeDtypeStruct(o.shape, o.dtype) for o in outs),
        in_specs=[pl.BlockSpec(memory_space=vmem)] * 3,
        out_specs=[pl.BlockSpec(memory_space=pl.ANY)] * 3,
        scratch_shapes=[pltpu.SemaphoreType.DMA((3,))],
    )(*[pltpu.with_memory_space_constraint(o, vmem) for o in outs])
    if gathered:
        def scatter(part):
            whole = lax.dynamic_update_slice_in_dim(jnp.zeros((channels, taps), F32), part, group * cg, 0)
            return lax.psum_scatter(whole, "seq", scatter_dimension=0, tiled=True)

        return outs[0], scatter(outs[1]), scatter(outs[2])
    return tuple(outs)


def solution(mesh):
    return jax.shard_map(
        per_device,
        mesh=mesh,
        in_specs=(
            P(("groups", "seq")),
            P(),
            P("seq", None),
            P("seq", None),
            P(("groups", "seq"), None),
        ),
        out_specs=(
            P(("groups", "seq"), None),
            P(("groups", "seq"), None),
            P(("groups", "seq"), None),
        ),
        check_vma=False,
    )
```

```python
import functools
import math

import jax
import jax.numpy as jnp
from jax import lax
from jax.experimental import pallas as pl
from jax.experimental.pallas import tpu as pltpu
from jax.sharding import PartitionSpec as P

GROUPS = 8
TAPS = 9
HALF = TAPS // 2
SPAN = TAPS + 1
LANES = 128
MESH = pl.DeviceIdType.MESH
F32 = jnp.float32
BF16 = jnp.bfloat16


def lane_contract(left, right):
    return lax.dot_general(left, right, (((1,), (1,)), ((), ())), preferred_element_type=F32)


def dot(left, right):
    return jnp.dot(left, right, preferred_element_type=F32)


def iota(shape, axis):
    return lax.broadcasted_iota(jnp.int32, shape, axis)


def split_halves(values):
    high = values.astype(BF16).astype(F32)
    return jnp.where((iota(values.shape, 1) & 7) < 4, high, values - high).astype(BF16)


def group_of(place):
    return place // 2 + (GROUPS // 2) * (place % 2)


def place_of(group):
    return (group % (GROUPS // 2)) * 2 + group // (GROUPS // 2)


def gelu_and_slope(pre):
    z = jnp.abs(pre) * math.sqrt(0.5)
    t = pl.reciprocal(1.0 + 0.3275911 * z)
    e = jnp.exp(-0.5 * pre * pre)
    series = 1.061405429
    for c in (-1.453152027, 1.421413741, -0.284496736, 0.254829592):
        series = series * t + c
    tail = (0.5 * series) * (t * e)
    cdf = jnp.where(pre < 0, tail, 1.0 - tail)
    return pre * cdf, cdf + pre * (e * (1.0 / math.sqrt(2.0 * math.pi)))


def block_kernel(
    count, members, gathered,
    bases_hbm, table_hbm, first_hbm, second_hbm, cot_hbm,
    comb_out, first_out, second_out,
    bases_ref, table_ref, first_ref, second_ref, cot_ref,
    diag_ref, skip_ref, codes_ref, cot_perm, cot_t, edges,
    codes_in, codes_left, codes_right, mix_send, mix_in, second_in,
    cot_in, cot_left, cot_right, comb_send, comb_in, s_send, s_in, t_send, t_in,
    onehot, hid, slope, unf, cot_unf, r_acc, lhs_out, lhs_grad,
    send_sems, recv_sems, load_sems,
):
    me = lax.axis_index("seq")
    chunk_of = me // GROUPS
    place = me % GROUPS
    group = group_of(place)
    chunks = count // GROUPS
    band = cot_ref.shape[0]
    cg = cot_in.shape[0]
    pair = 2 * cg
    taps = TAPS * cg
    span = SPAN * cg
    deep = span + 64
    half = band // 2
    q = half * GROUPS
    width = q + LANES
    channels = GROUPS * cg
    rows = cg if gathered else cg // members
    owner = me // members
    member = me % members
    started = []

    def push(src, dst, kind, recv, target, here=None):
        remote = pltpu.make_async_remote_copy(
            src_ref=src, dst_ref=dst, send_sem=send_sems.at[kind], recv_sem=recv_sems.at[recv],
            device_id={"seq": target}, device_id_type=MESH,
        )
        away = target != me
        if here is not None:
            away = here & away
            local = here & (target == me)
        else:
            local = target == me

        @pl.when(away)
        def _():
            remote.start()

        @pl.when(local)
        def _():
            pltpu.make_async_copy(src, dst, recv_sems.at[recv]).start()

        started.append((remote, away))

    def arrived(ref, recv):
        pltpu.make_async_copy(ref, ref, recv_sems.at[recv]).wait()

    def push_chunk(src_of, dst, kind, recv):
        for k in range(GROUPS):
            to = (place + k + 1) % GROUPS
            push(src_of(to), dst, kind, recv, chunk_of * GROUPS + to)

    def push_edges(src_of, left_dst, right_dst, kind, recv_left, recv_right):
        for low, dst, recv, here, there in (
            (True, right_dst, recv_right, (place == 0) & (chunk_of > 0), chunk_of - 1),
            (False, left_dst, recv_left, (place == GROUPS - 1) & (chunk_of < chunks - 1), chunk_of + 1),
        ):
            for to in range(GROUPS):
                push(src_of(to, low), dst, kind, recv, there * GROUPS + to, here)

    def edges_arrived(left, right, recv_left, recv_right):
        @pl.when(chunk_of > 0)
        def _():
            arrived(left, recv_left)

        @pl.when(chunk_of < chunks - 1)
        def _():
            arrived(right, recv_right)

    barrier = pltpu.get_barrier_semaphore()
    for k in range(1, count):
        pl.semaphore_signal(barrier, inc=1, device_id={"seq": (me + k) % count}, device_id_type=MESH)

    loads = [
        pltpu.make_async_copy(src, dst, load_sems.at[k])
        for k, (src, dst) in enumerate(
            (
                (bases_hbm, bases_ref), (table_hbm, table_ref), (first_hbm, first_ref),
                (cot_hbm, cot_ref), (second_hbm, second_ref),
            )
        )
    ]
    for load in loads:
        load.start()

    spread = (iota((band, band), 1) == 2 * (iota((band, band), 0) % half) + iota((band, band), 0) // half)
    spread = spread.astype(F32).astype(BF16)
    loads[0].wait()
    bases = jnp.broadcast_to(bases_ref[...], (8, band)).astype(F32).astype(BF16)
    codes = lane_contract(bases, spread)
    codes_ref[...] = jnp.concatenate([codes[:, :half], codes[:, half:]], axis=0).astype(BF16)

    loads[1].wait()
    table = table_ref[...].astype(F32)
    code = iota((8, channels), 0)
    wide = jnp.zeros((8, channels), F32)
    turned = jnp.zeros((8, channels), F32)
    for c in range(4):
        wide = jnp.where(code % 4 == c, table[c : c + 1], wide)
        turned = jnp.where(code == 7 - c, table[c : c + 1], turned)
    lane = iota((8, channels), 1)
    whose = group if gathered else owner
    strand = jnp.where(lane < cg, pltpu.roll(wide, (channels - whose * cg) % channels, 1), 0.0)
    strand = jnp.concatenate([strand, jnp.zeros((8, LANES), F32)], axis=1)
    diag_ref[...] = jnp.concatenate([pltpu.roll(strand, cg * t, 1) for t in range(TAPS)], axis=0)[:, :taps].astype(BF16)
    own = pltpu.roll(jnp.where(code < 4, wide, turned), (channels - group * cg) % channels, 1)[:, :cg]
    eye = (iota((band, band), 0) == iota((band, band), 1)).astype(F32).astype(BF16)
    skip_ref[...] = lane_contract(
        eye[:cg, :cg],
        jnp.concatenate([own, jnp.zeros((8, cg), F32)], axis=0).astype(BF16),
    ).astype(BF16)
    loads[2].wait()
    mix = split_halves(lane_contract(first_ref[...], diag_ref[...]))
    if gathered:
        mix_in[0, :, : 8 * TAPS] = mix
    else:
        mix_send[:, : 8 * TAPS] = mix

    loads[3].wait()
    for j in range(channels // band):
        cot_perm[:, band * j : band * (j + 1)] = dot(
            spread, cot_ref[:, band * j : band * (j + 1)]
        ).astype(BF16)
    for j in range(channels // band):
        cot_t[band * j : band * (j + 1)] = lane_contract(
            eye, cot_perm[:, band * j : band * (j + 1)]
        ).astype(BF16)
    for to in range(GROUPS):
        g = group_of(to)
        for b in range(2):
            edges[0, to, b] = cot_perm[half * b : half * b + 16, cg * g : cg * (g + 1)]
            edges[1, to, b] = cot_perm[half * (b + 1) - 16 : half * (b + 1), cg * g : cg * (g + 1)]

    loads[4].wait()
    pl.semaphore_wait(barrier, count - 1)

    here = pl.ds(pl.multiple_of(place * half, LANES), half)
    push_chunk(lambda to: codes_ref, codes_in.at[:, here], 0, 0)
    push_edges(lambda to, low: codes_ref, codes_left, codes_right, 1, 1, 2)
    if not gathered:
        for c in range(chunks):
            push(mix_send, mix_in.at[member], 2, 3, c * GROUPS + place_of(owner))
    if not gathered:
        for c in range(1, chunks + 1):
            push(second_ref, second_in.at[member], 3, 4, (chunk_of + c) % chunks * GROUPS + place_of(owner))
    here = pl.ds(pl.multiple_of(place * band, LANES), band)
    push_chunk(
        lambda to: cot_t.at[pl.ds(pl.multiple_of(group_of(to) * cg, 16), cg)], cot_in.at[:, here], 4, 5
    )
    push_edges(lambda to, low: edges.at[0 if low else 1, to], cot_left, cot_right, 5, 6, 7)

    has_right = (chunk_of < chunks - 1).astype(jnp.int32)
    has_left = (chunk_of > 0).astype(jnp.int32)

    def edge_mask(height):
        lane = iota((height, LANES), 1)
        return lane < LANES // 2, jnp.where(lane < LANES // 2, has_right, has_left) > 0

    for a in range(2):
        for s in range(2):
            hid[a, LANES * s + cg : LANES * (s + 1), :] = jnp.zeros((LANES - cg, width), BF16)
    arrived(codes_in, 0)
    edges_arrived(codes_left, codes_right, 1, 2)
    on_right, real = edge_mask(16)
    edge = jnp.where(real, jnp.where(on_right, codes_right[...].astype(F32), codes_left[...].astype(F32)), 4.0)
    codes = jnp.concatenate([codes_in[...].astype(F32), edge], axis=1)
    want = (iota((8, width), 0) & 3).astype(F32)
    moved = {}
    for b in range(2):
        for s in range(-2, 3):
            line = codes[8 * b : 8 * (b + 1)]
            moved[s, b] = line if s == 0 else pltpu.roll(line, (-s) % width, 1)
    for strand in range(2):
        blocks = []
        for j in range(SPAN):
            value = moved[j // 2 - 2, j % 2] if strand == 0 else 3.0 - moved[2 - j // 2, 1 - j % 2]
            blocks.append(jnp.where(value == want, 1.0, 0.0))
        onehot[strand] = jnp.concatenate(blocks, axis=0).astype(BF16)
    for strand in range(2):
        top = strand * deep + span
        unf[top : top + 16, :] = onehot[0, 8 * HALF : 8 * HALF + 16, :q]

    if not gathered:
        arrived(mix_in, 3)
    mix = mix_in[...].reshape(cg, LANES).astype(F32)
    mix = jnp.where(iota((cg, LANES), 1) < 8 * TAPS, mix, 0.0)
    mix = jnp.concatenate([mix, pltpu.roll(mix, 8, 1)], axis=0)[:, : 8 * SPAN].astype(BF16)

    def store_hidden(strand, cols, hidden):
        for k in range(2):
            hid[k if strand == 0 else 1 - k, LANES * strand : LANES * strand + cg, cols] = hidden[cg * k : cg * (k + 1)]

    def activate(cols):
        for strand in range(2):
            hidden, grad = gelu_and_slope(dot(mix, onehot[strand, :, cols]))
            store_hidden(strand, cols, hidden.astype(BF16))
            slope[pair * strand : pair * (strand + 1), cols] = grad

    def unfold(i):
        for b in range(2):
            for strand in range(2):
                rows_at = slice(LANES * strand, LANES * strand + cg)
                low = 256 * i - LANES
                if low < 0:
                    line = jnp.concatenate([hid[b, rows_at, q:], hid[b, rows_at, : 256 + LANES]], axis=1)
                else:
                    line = hid[b, rows_at, low : low + 512]
                for s in range(-2, 3):
                    j = 2 * (s + 2) + b if strand == 0 else 2 * (2 - s) + 1 - b
                    top = strand * deep + cg * j
                    moved = line if s == 0 else pltpu.roll(line, (-s) % 512, 1)
                    unf[top : top + cg, 256 * i : 256 * (i + 1)] = moved[:, LANES : LANES + 256]

    _, real = edge_mask(pair)
    for strand in range(2):
        hidden, _ = gelu_and_slope(dot(mix, onehot[strand, :, q:]))
        store_hidden(strand, slice(q, width), jnp.where(real, hidden, 0.0).astype(BF16))
    blocks = q // 256
    for i in range(blocks):
        activate(slice(256 * i, 256 * (i + 1)))
        if i > 0:
            unfold(i - 1)
    unfold(blocks - 1)

    if gathered:
        second = second_ref[...]
    else:
        arrived(second_in, 4)
        second = second_in[...].reshape(cg, taps)
    own = jnp.concatenate([skip_ref[...], jnp.zeros((cg, LANES - 16), BF16)], axis=1).astype(F32)
    part = jnp.concatenate([second, jnp.zeros((cg, deep - taps), BF16)], axis=1).astype(F32)
    lag = pltpu.roll(part, cg, 1)
    for strand in range(2):
        x = jnp.where(iota((cg, LANES), 1) // 4 == strand, own, 0.0)
        x = jnp.concatenate([jnp.zeros((cg, deep - LANES), F32), pltpu.roll(x, LANES // 2, 1)], axis=1)
        at = slice(deep * strand, deep * (strand + 1))
        lhs_out[0:cg, at] = ((part, lag)[strand] + x).astype(BF16)
        lhs_out[cg:, at] = ((lag, part)[strand] + pltpu.roll(x, 8, 1)).astype(BF16)

    steps = GROUPS // 2
    for k in range(steps):
        pick = (place // 2 + 1 + k) % steps
        cols = pl.ds(pl.multiple_of(pick * band, LANES), band)
        out, back = (
            dot(lhs_out[:, deep * strand : deep * strand + span + 16], unf[deep * strand : deep * strand + span + 16, cols])
            for strand in range(2)
        )
        out = (out + back.astype(BF16).astype(F32)).astype(BF16)
        comb_send[:, pl.ds(pl.multiple_of(2 * pick * band, LANES), 2 * band)] = jnp.concatenate(
            [out[cg * a : cg * (a + 1), half * b : half * (b + 1)] for b in range(2) for a in range(2)], axis=1
        )
        for b in range(2):
            side = (place + 1 + b) % 2
            at = pl.ds(pl.multiple_of((2 * pick + side) * band, LANES), band)
            if k == steps - 1 and b == 1:
                pltpu.make_async_copy(comb_send.at[:, at], comb_in.at[group], recv_sems.at[8]).start()
            else:
                remote = pltpu.make_async_remote_copy(
                    src_ref=comb_send.at[:, at], dst_ref=comb_in.at[group], send_sem=send_sems.at[6],
                    recv_sem=recv_sems.at[8], device_id={"seq": chunk_of * GROUPS + 2 * pick + side},
                    device_id_type=MESH,
                )
                remote.start()
                started.append((remote, None))

    arrived(cot_in, 5)
    even, odd = (
        jnp.concatenate([cot_in[:, band * k + half * b : band * k + half * (b + 1)] for k in range(GROUPS)], axis=1)
        for b in range(2)
    )
    forward = jnp.concatenate([even, odd], axis=0)
    reverse = jnp.concatenate([odd, even], axis=0)
    parts = tuple(range(0, span, 256)) + (span,)
    done = 0
    for low, high in zip(parts[:-1], parts[1:]):
        for n in range(low, high, 256):
            size = min(256, high - n)
            r_acc[:, n : n + size] = lane_contract(forward, unf[n : n + size, :]) + lane_contract(
                reverse, unf[deep + n : deep + n + size, :]
            )
        end = taps if high == span else (high - cg) // LANES * LANES
        near = slice(done, min(r_acc.shape[1], -(-(end + cg) // LANES) * LANES))
        height = near.stop - near.start
        total = r_acc[0:cg, done:end] + pltpu.roll(r_acc[cg:, near], height - cg, 1)[:, : end - done]
        if gathered:
            s_in[0, :, done:end] = total.astype(BF16)
        else:
            at = slice(done, min(s_send.shape[2], -(-end // LANES) * LANES))
            for k in range(members):
                s_send[k, :, done:end] = total[rows * k : rows * (k + 1)].astype(BF16)
            for k in range(members):
                push(
                    s_send.at[k, :, pl.ds(at.start, at.stop - at.start)],
                    s_in.at[chunk_of, :, pl.ds(at.start, at.stop - at.start)], 7, 9, group * members + k,
                )
        done = end

    stack = []
    for t in range(SPAN):
        lowered = second[:, cg * (8 - t) : cg * (9 - t)] if t < TAPS else jnp.zeros((cg, cg), BF16)
        raised = second[:, cg * (9 - t) : cg * (10 - t)] if t > 0 else jnp.zeros((cg, cg), BF16)
        before = second[:, cg * (t - 1) : cg * t] if t > 0 else jnp.zeros((cg, cg), BF16)
        after = second[:, cg * t : cg * (t + 1)] if t < TAPS else jnp.zeros((cg, cg), BF16)
        stack.append(jnp.concatenate([lowered, raised, before, after], axis=1))
    stack = jnp.concatenate(stack, axis=0)
    for strand in range(2):
        lhs_grad[pair * strand : pair * (strand + 1)] = lane_contract(
            eye[:pair, :pair], stack[:, pair * strand : pair * (strand + 1)]
        ).astype(BF16)

    edges_arrived(cot_left, cot_right, 6, 7)
    for b in range(2):
        edge = lane_contract(
            eye[:cg, :cg],
            jnp.concatenate(
                [
                    jnp.where(has_right > 0, cot_right[b].astype(F32), 0.0),
                    jnp.zeros((LANES - 32, cg), F32),
                    jnp.where(has_left > 0, cot_left[b].astype(F32), 0.0),
                ],
                axis=0,
            ).astype(BF16),
        ).astype(BF16)
        line = jnp.concatenate(
            [cot_in[:, band * k + half * b : band * k + half * (b + 1)] for k in range(GROUPS)] + [edge], axis=1
        )
        for s in range(-2, 3):
            top = cg * (2 * (s + 2) + b)
            cot_unf[top : top + cg, :] = (line if s == 0 else pltpu.roll(line, (-s) % width, 1))[:, :q]

    def backward(i, total):
        cols = pl.ds(pl.multiple_of(i * 256, 256), 256)
        grad = dot(lhs_grad[...], cot_unf[:, cols])
        pre_grad = (grad * slope[:, cols]).astype(BF16)
        return (
            total
            + lane_contract(pre_grad[:pair], onehot[0, :, cols])
            + lane_contract(pre_grad[pair:], onehot[1, :, cols])
        )

    terms = lax.fori_loop(0, q // 256, backward, jnp.zeros((pair, 8 * SPAN), F32), unroll=True)
    shifted = jnp.concatenate([terms[cg:], jnp.zeros((cg, LANES - 8 * SPAN), F32)], axis=1)
    terms = terms[:cg, : 8 * TAPS] + pltpu.roll(shifted, LANES - 8, 1)[:, : 8 * TAPS]
    if gathered:
        t_in[0, :, : 8 * TAPS] = terms
    else:
        for k in range(members):
            t_send[k, :, : 8 * TAPS] = terms[rows * k : rows * (k + 1)]
        for k in range(members):
            push(t_send.at[k], t_in.at[chunk_of], 8, 10, group * members + k)

    arrived(comb_in, 8)
    for j in range(channels // band):
        part = comb_in[...].reshape(channels, band)[band * j : band * (j + 1)]
        gather = (iota((band, band), 1) == (iota((band, band), 0) % 2) * half + iota((band, band), 0) // 2)
        comb_out[:, band * j : band * (j + 1)] = lane_contract(gather.astype(F32).astype(BF16), part).astype(BF16)
    if not gathered:
        arrived(s_in, 9)
    second_out[...] = jnp.sum(s_in[:, :, :taps].astype(F32), axis=0)
    if not gathered:
        arrived(t_in, 10)
    first_out[...] = dot(split_halves(jnp.sum(t_in[:, :, : 8 * TAPS], axis=0)), diag_ref[...])

    for remote, away in started:
        if away is None:
            remote.wait_send()
            continue

        @pl.when(away)
        def _():
            remote.wait_send()


def finish_kernel(*refs):
    sems = refs[6]
    copies = [pltpu.make_async_copy(refs[k], refs[3 + k], sems.at[k]) for k in range(3)]
    for copy in copies:
        copy.start()
    for copy in copies:
        copy.wait()


def per_device(bases, base_table, first_kernel, second_kernel, cotangent):
    band, channels = cotangent.shape
    cg = channels // GROUPS
    count = lax.axis_size("seq")
    members = count // GROUPS
    rows = first_kernel.shape[0]
    gathered = rows % 16 != 0
    half = band // 2
    q = half * GROUPS
    width = q + LANES
    pair = 2 * cg
    taps = TAPS * cg
    span = SPAN * cg
    deep = 2 * (span + 64)

    lot = 1 if gathered else members
    if gathered:
        group = group_of(lax.axis_index("seq") % GROUPS)
        first_kernel, second_kernel = (
            lax.dynamic_slice_in_dim(lax.all_gather(k, "seq", axis=0, tiled=True), group * cg, cg, 0)
            for k in (first_kernel, second_kernel)
        )
        rows = cg

    vmem = pltpu.VMEM
    outs = pl.pallas_call(
        functools.partial(block_kernel, count, members, gathered),
        out_shape=(
            vmem((band, channels), BF16),
            vmem((rows, taps), F32),
            vmem((rows, taps), F32),
        ),
        in_specs=[pl.BlockSpec(memory_space=pl.ANY)] * 5,
        out_specs=[pl.BlockSpec(memory_space=vmem)] * 3,
        scratch_shapes=[
            vmem((1, band), jnp.int32),
            vmem(base_table.shape, BF16),
            vmem(first_kernel.shape, BF16),
            vmem(second_kernel.shape, BF16),
            vmem((band, channels), BF16),
            vmem((8 * TAPS, taps), BF16),
            vmem((cg, 16), BF16),
            vmem((16, half), BF16),
            vmem((band, channels), BF16),
            vmem((channels, band), BF16),
            vmem((2, GROUPS, 2, 16, cg), BF16),
            vmem((16, q), BF16),
            vmem((16, LANES), BF16),
            vmem((16, LANES), BF16),
            vmem((rows, LANES), BF16),
            vmem((lot, rows, LANES), BF16),
            vmem((lot, rows, taps), BF16),
            vmem((cg, 2 * q), BF16),
            vmem((2, 16, cg), BF16),
            vmem((2, 16, cg), BF16),
            vmem((cg, 2 * q), BF16),
            vmem((GROUPS, cg, band), BF16),
            vmem((lot, rows, -(-taps // LANES) * LANES), BF16),
            vmem((lot, rows, -(-taps // LANES) * LANES), BF16),
            vmem((lot, rows, LANES), F32),
            vmem((lot, rows, LANES), F32),
            vmem((2, 8 * SPAN, width), BF16),
            vmem((2, 2 * LANES, width), BF16),
            vmem((2 * pair, q), F32),
            vmem((deep, q), BF16),
            vmem((span, q), BF16),
            vmem((pair, span + 64), F32),
            vmem((pair, deep), BF16),
            vmem((2 * pair, span), BF16),
            pltpu.SemaphoreType.DMA((9,)),
            pltpu.SemaphoreType.DMA((11,)),
            pltpu.SemaphoreType.DMA((5,)),
        ],
        compiler_params=pltpu.CompilerParams(
            collective_id=0, has_side_effects=True, vmem_limit_bytes=56 * 1024 * 1024
        ),
    )(bases.reshape(1, band), base_table, first_kernel, second_kernel, cotangent)

    outs = pl.pallas_call(
        finish_kernel,
        out_shape=tuple(jax.ShapeDtypeStruct(o.shape, o.dtype) for o in outs),
        in_specs=[pl.BlockSpec(memory_space=vmem)] * 3,
        out_specs=[pl.BlockSpec(memory_space=pl.ANY)] * 3,
        scratch_shapes=[pltpu.SemaphoreType.DMA((3,))],
    )(*[pltpu.with_memory_space_constraint(o, vmem) for o in outs])
    if gathered:
        def scatter(part):
            whole = lax.dynamic_update_slice_in_dim(jnp.zeros((channels, taps), F32), part, group * cg, 0)
            return lax.psum_scatter(whole, "seq", scatter_dimension=0, tiled=True)

        return outs[0], scatter(outs[1]), scatter(outs[2])
    return tuple(outs)


def solution(mesh):
    return jax.shard_map(
        per_device,
        mesh=mesh,
        in_specs=(
            P(("groups", "seq")),
            P(),
            P("seq", None),
            P("seq", None),
            P(("groups", "seq"), None),
        ),
        out_specs=(
            P(("groups", "seq"), None),
            P(("groups", "seq"), None),
            P(("groups", "seq"), None),
        ),
        check_vma=False,
    )
```

```python
import functools
import math

import jax
import jax.numpy as jnp
from jax import lax
from jax.experimental import pallas as pl
from jax.experimental.pallas import tpu as pltpu
from jax.sharding import PartitionSpec as P

GROUPS = 8
TAPS = 9
HALF = TAPS // 2
SPAN = TAPS + 1
LANES = 128
MESH = pl.DeviceIdType.MESH
F32 = jnp.float32
BF16 = jnp.bfloat16


def lane_contract(left, right):
    return lax.dot_general(left, right, (((1,), (1,)), ((), ())), preferred_element_type=F32)


def dot(left, right):
    return jnp.dot(left, right, preferred_element_type=F32)


def iota(shape, axis):
    return lax.broadcasted_iota(jnp.int32, shape, axis)


def split_halves(values):
    high = values.astype(BF16).astype(F32)
    return jnp.where((iota(values.shape, 1) & 7) < 4, high, values - high).astype(BF16)


def group_of(place):
    return place // 2 + (GROUPS // 2) * (place % 2)


def place_of(group):
    return (group % (GROUPS // 2)) * 2 + group // (GROUPS // 2)


def gelu_and_slope(pre):
    z = jnp.abs(pre) * math.sqrt(0.5)
    t = pl.reciprocal(1.0 + 0.3275911 * z)
    e = jnp.exp(-0.5 * pre * pre)
    series = 1.061405429
    for c in (-1.453152027, 1.421413741, -0.284496736, 0.254829592):
        series = series * t + c
    tail = (0.5 * series) * (t * e)
    cdf = jnp.where(pre < 0, tail, 1.0 - tail)
    return pre * cdf, cdf + pre * (e * (1.0 / math.sqrt(2.0 * math.pi)))


def block_kernel(
    count, members, gathered,
    bases_hbm, table_hbm, first_hbm, second_hbm, cot_hbm,
    comb_out, first_out, second_out,
    bases_ref, table_ref, first_ref, second_ref, cot_ref,
    diag_ref, skip_ref, codes_ref, cot_perm, cot_t, edges,
    codes_in, codes_left, codes_right, mix_send, mix_in, second_in,
    cot_in, cot_left, cot_right, comb_send, comb_in, s_send, s_in, t_send, t_in,
    onehot, hid, slope, unf, cot_unf, r_acc, lhs_out, lhs_grad,
    send_sems, recv_sems, load_sems,
):
    me = lax.axis_index("seq")
    chunk_of = me // GROUPS
    place = me % GROUPS
    group = group_of(place)
    chunks = count // GROUPS
    band = cot_ref.shape[0]
    cg = cot_in.shape[0]
    pair = 2 * cg
    taps = TAPS * cg
    span = SPAN * cg
    deep = span + 64
    half = band // 2
    q = half * GROUPS
    width = q + LANES
    channels = GROUPS * cg
    rows = cg if gathered else cg // members
    owner = me // members
    member = me % members
    started = []

    def push(src, dst, kind, recv, target, here=None):
        remote = pltpu.make_async_remote_copy(
            src_ref=src, dst_ref=dst, send_sem=send_sems.at[kind], recv_sem=recv_sems.at[recv],
            device_id={"seq": target}, device_id_type=MESH,
        )
        away = target != me
        if here is not None:
            away = here & away
            local = here & (target == me)
        else:
            local = target == me

        @pl.when(away)
        def _():
            remote.start()

        @pl.when(local)
        def _():
            pltpu.make_async_copy(src, dst, recv_sems.at[recv]).start()

        started.append((remote, away))

    def arrived(ref, recv):
        pltpu.make_async_copy(ref, ref, recv_sems.at[recv]).wait()

    def push_chunk(src_of, dst, kind, recv):
        for k in range(GROUPS):
            to = (place + k + 1) % GROUPS
            push(src_of(to), dst, kind, recv, chunk_of * GROUPS + to)

    def push_edges(src_of, left_dst, right_dst, kind, recv_left, recv_right):
        for low, dst, recv, here, there in (
            (True, right_dst, recv_right, (place == 0) & (chunk_of > 0), chunk_of - 1),
            (False, left_dst, recv_left, (place == GROUPS - 1) & (chunk_of < chunks - 1), chunk_of + 1),
        ):
            for to in range(GROUPS):
                push(src_of(to, low), dst, kind, recv, there * GROUPS + to, here)

    def edges_arrived(left, right, recv_left, recv_right):
        @pl.when(chunk_of > 0)
        def _():
            arrived(left, recv_left)

        @pl.when(chunk_of < chunks - 1)
        def _():
            arrived(right, recv_right)

    barrier = pltpu.get_barrier_semaphore()
    for k in range(1, count):
        pl.semaphore_signal(barrier, inc=1, device_id={"seq": (me + k) % count}, device_id_type=MESH)

    loads = [
        pltpu.make_async_copy(src, dst, load_sems.at[k])
        for k, (src, dst) in enumerate(
            (
                (bases_hbm, bases_ref), (table_hbm, table_ref), (first_hbm, first_ref),
                (cot_hbm, cot_ref), (second_hbm, second_ref),
            )
        )
    ]
    for load in loads:
        load.start()

    spread = (iota((band, band), 1) == 2 * (iota((band, band), 0) % half) + iota((band, band), 0) // half)
    spread = spread.astype(F32).astype(BF16)
    loads[0].wait()
    bases = jnp.broadcast_to(bases_ref[...], (8, band)).astype(F32).astype(BF16)
    codes = lane_contract(bases, spread)
    codes_ref[...] = codes[0:1]

    loads[1].wait()
    table = table_ref[...].astype(F32)
    code = iota((8, channels), 0)
    wide = jnp.zeros((8, channels), F32)
    turned = jnp.zeros((8, channels), F32)
    for c in range(4):
        wide = jnp.where(code % 4 == c, table[c : c + 1], wide)
        turned = jnp.where(code == 7 - c, table[c : c + 1], turned)
    lane = iota((8, channels), 1)
    whose = group if gathered else owner
    strand = jnp.where(lane < cg, pltpu.roll(wide, (channels - whose * cg) % channels, 1), 0.0)
    strand = jnp.concatenate([strand, jnp.zeros((8, LANES), F32)], axis=1)
    diag_ref[...] = jnp.concatenate([pltpu.roll(strand, cg * t, 1) for t in range(TAPS)], axis=0)[:, :taps].astype(BF16)
    own = pltpu.roll(jnp.where(code < 4, wide, turned), (channels - group * cg) % channels, 1)[:, :cg]
    eye = (iota((band, band), 0) == iota((band, band), 1)).astype(F32).astype(BF16)
    skip_ref[...] = lane_contract(
        eye[:cg, :cg],
        jnp.concatenate([own, jnp.zeros((8, cg), F32)], axis=0).astype(BF16),
    ).astype(BF16)
    loads[2].wait()
    mix = split_halves(lane_contract(first_ref[...], diag_ref[...]))
    if gathered:
        mix_in[0, :, : 8 * TAPS] = mix
    else:
        mix_send[:, : 8 * TAPS] = mix

    loads[3].wait()
    for j in range(channels // band):
        cot_perm[:, band * j : band * (j + 1)] = dot(
            spread, cot_ref[:, band * j : band * (j + 1)]
        ).astype(BF16)
    for j in range(channels // band):
        cot_t[band * j : band * (j + 1)] = lane_contract(
            eye, cot_perm[:, band * j : band * (j + 1)]
        ).astype(BF16)
    for to in range(GROUPS):
        g = group_of(to)
        lanes = slice(cg * g, cg * (g + 1))
        edges[0, to] = jnp.concatenate([cot_perm[half * b : half * b + 8, lanes] for b in range(2)], axis=0)
        edges[1, to] = jnp.concatenate([cot_perm[half * (b + 1) - 8 : half * (b + 1), lanes] for b in range(2)], axis=0)

    loads[4].wait()
    pl.semaphore_wait(barrier, count - 1)

    here = pl.ds(pl.multiple_of(place * band, LANES), band)
    push_chunk(lambda to: codes_ref, codes_in.at[:, here], 0, 0)
    push_edges(lambda to, low: codes_ref, codes_left, codes_right, 1, 1, 2)
    if not gathered:
        for c in range(chunks):
            push(mix_send, mix_in.at[member], 2, 3, c * GROUPS + place_of(owner))
    if not gathered:
        for c in range(1, chunks + 1):
            push(second_ref, second_in.at[member], 3, 4, (chunk_of + c) % chunks * GROUPS + place_of(owner))
    here = pl.ds(pl.multiple_of(place * band, LANES), band)
    push_chunk(
        lambda to: cot_t.at[pl.ds(pl.multiple_of(group_of(to) * cg, 16), cg)], cot_in.at[:, here], 4, 5
    )
    push_edges(lambda to, low: edges.at[0 if low else 1, to], cot_left, cot_right, 5, 6, 7)

    has_right = (chunk_of < chunks - 1).astype(jnp.int32)
    has_left = (chunk_of > 0).astype(jnp.int32)

    def edge_mask(height):
        lane = iota((height, LANES), 1)
        return lane < LANES // 2, jnp.where(lane < LANES // 2, has_right, has_left) > 0

    for a in range(2):
        for s in range(2):
            hid[a, LANES * s + cg : LANES * (s + 1), :] = jnp.zeros((LANES - cg, width), BF16)
    arrived(codes_in, 0)
    edges_arrived(codes_left, codes_right, 1, 2)
    on_right, real = edge_mask(1)
    lines = []
    for b in range(2):
        edge = jnp.where(on_right, codes_right[:, half * b : half * b + LANES], codes_left[:, half * (b + 1) - LANES : half * (b + 1)])
        line = [codes_in[:, band * k + half * b : band * k + half * (b + 1)] for k in range(GROUPS)]
        lines.append(jnp.broadcast_to(jnp.concatenate(line + [jnp.where(real, edge, 4.0)], axis=1), (8, width)))
    want = (iota((8, width), 0) & 3).astype(F32)
    moved = {}
    for b in range(2):
        for s in range(-2, 3):
            moved[s, b] = lines[b] if s == 0 else pltpu.roll(lines[b], (-s) % width, 1)
    for strand in range(2):
        blocks = []
        for j in range(SPAN):
            value = moved[j // 2 - 2, j % 2] if strand == 0 else 3.0 - moved[2 - j // 2, 1 - j % 2]
            blocks.append(jnp.where(value == want, 1.0, 0.0))
        onehot[strand] = jnp.concatenate(blocks, axis=0).astype(BF16)
    for strand in range(2):
        top = strand * deep + span
        unf[top : top + 16, :] = onehot[0, 8 * HALF : 8 * HALF + 16, :q]

    if not gathered:
        arrived(mix_in, 3)
    mix = mix_in[...].reshape(cg, LANES).astype(F32)
    mix = jnp.where(iota((cg, LANES), 1) < 8 * TAPS, mix, 0.0)
    mix = jnp.concatenate([mix, pltpu.roll(mix, 8, 1)], axis=0)[:, : 8 * SPAN].astype(BF16)

    def store_hidden(strand, cols, hidden):
        for k in range(2):
            hid[k if strand == 0 else 1 - k, LANES * strand : LANES * strand + cg, cols] = hidden[cg * k : cg * (k + 1)]

    def activate(cols):
        for strand in range(2):
            hidden, grad = gelu_and_slope(dot(mix, onehot[strand, :, cols]))
            store_hidden(strand, cols, hidden.astype(BF16))
            slope[pair * strand : pair * (strand + 1), cols] = grad

    def unfold(i):
        for b in range(2):
            for strand in range(2):
                rows_at = slice(LANES * strand, LANES * strand + cg)
                low = 256 * i - LANES
                if low < 0:
                    line = jnp.concatenate([hid[b, rows_at, q:], hid[b, rows_at, : 256 + LANES]], axis=1)
                else:
                    line = hid[b, rows_at, low : low + 512]
                for s in range(-2, 3):
                    j = 2 * (s + 2) + b if strand == 0 else 2 * (2 - s) + 1 - b
                    top = strand * deep + cg * j
                    moved = line if s == 0 else pltpu.roll(line, (-s) % 512, 1)
                    unf[top : top + cg, 256 * i : 256 * (i + 1)] = moved[:, LANES : LANES + 256]

    _, real = edge_mask(pair)
    for strand in range(2):
        hidden, _ = gelu_and_slope(dot(mix, onehot[strand, :, q:]))
        store_hidden(strand, slice(q, width), jnp.where(real, hidden, 0.0).astype(BF16))
    blocks = q // 256
    for i in range(blocks):
        activate(slice(256 * i, 256 * (i + 1)))
        if i > 0:
            unfold(i - 1)
    unfold(blocks - 1)

    if gathered:
        second = second_ref[...]
    else:
        arrived(second_in, 4)
        second = second_in[...].reshape(cg, taps)
    own = jnp.concatenate([skip_ref[...], jnp.zeros((cg, LANES - 16), BF16)], axis=1).astype(F32)
    part = jnp.concatenate([second, jnp.zeros((cg, deep - taps), BF16)], axis=1).astype(F32)
    lag = pltpu.roll(part, cg, 1)
    for strand in range(2):
        x = jnp.where(iota((cg, LANES), 1) // 4 == strand, own, 0.0)
        x = jnp.concatenate([jnp.zeros((cg, deep - LANES), F32), pltpu.roll(x, LANES // 2, 1)], axis=1)
        at = slice(deep * strand, deep * (strand + 1))
        lhs_out[0:cg, at] = ((part, lag)[strand] + x).astype(BF16)
        lhs_out[cg:, at] = ((lag, part)[strand] + pltpu.roll(x, 8, 1)).astype(BF16)

    steps = GROUPS // 2

    def send_outputs(k):
        pick = (place // 2 + 1 + k) % steps
        cols = pl.ds(pl.multiple_of(pick * band, LANES), band)
        out, back = (
            dot(lhs_out[:, deep * strand : deep * strand + span + 16], unf[deep * strand : deep * strand + span + 16, cols])
            for strand in range(2)
        )
        out = (out + back.astype(BF16).astype(F32)).astype(BF16)
        comb_send[:, pl.ds(pl.multiple_of(2 * pick * band, LANES), 2 * band)] = jnp.concatenate(
            [out[cg * a : cg * (a + 1), half * b : half * (b + 1)] for b in range(2) for a in range(2)], axis=1
        )
        for b in range(2):
            side = (place + 1 + b) % 2
            at = pl.ds(pl.multiple_of((2 * pick + side) * band, LANES), band)
            if k == steps - 1 and b == 1:
                pltpu.make_async_copy(comb_send.at[:, at], comb_in.at[group], recv_sems.at[8]).start()
            else:
                remote = pltpu.make_async_remote_copy(
                    src_ref=comb_send.at[:, at], dst_ref=comb_in.at[group], send_sem=send_sems.at[6],
                    recv_sem=recv_sems.at[8], device_id={"seq": chunk_of * GROUPS + 2 * pick + side},
                    device_id_type=MESH,
                )
                remote.start()
                started.append((remote, None))

    for k in range(2):
        send_outputs(k)

    stack = []
    for t in range(SPAN):
        lowered = second[:, cg * (8 - t) : cg * (9 - t)] if t < TAPS else jnp.zeros((cg, cg), BF16)
        raised = second[:, cg * (9 - t) : cg * (10 - t)] if t > 0 else jnp.zeros((cg, cg), BF16)
        before = second[:, cg * (t - 1) : cg * t] if t > 0 else jnp.zeros((cg, cg), BF16)
        after = second[:, cg * t : cg * (t + 1)] if t < TAPS else jnp.zeros((cg, cg), BF16)
        stack.append(jnp.concatenate([lowered, raised, before, after], axis=1))
    stack = jnp.concatenate(stack, axis=0)
    for strand in range(2):
        lhs_grad[pair * strand : pair * (strand + 1)] = lane_contract(
            eye[:pair, :pair], stack[:, pair * strand : pair * (strand + 1)]
        ).astype(BF16)

    arrived(cot_in, 5)
    even, odd = (
        jnp.concatenate([cot_in[:, band * k + half * b : band * k + half * (b + 1)] for k in range(GROUPS)], axis=1)
        for b in range(2)
    )
    forward = jnp.concatenate([even, odd], axis=0)
    reverse = jnp.concatenate([odd, even], axis=0)
    parts = tuple(range(0, span, 256)) + (span,)
    done = 0
    for low, high in zip(parts[:-1], parts[1:]):
        for n in range(low, high, 256):
            size = min(256, high - n)
            r_acc[:, n : n + size] = lane_contract(forward, unf[n : n + size, :]) + lane_contract(
                reverse, unf[deep + n : deep + n + size, :]
            )
        end = taps if high == span else (high - cg) // LANES * LANES
        near = slice(done, min(r_acc.shape[1], -(-(end + cg) // LANES) * LANES))
        height = near.stop - near.start
        total = r_acc[0:cg, done:end] + pltpu.roll(r_acc[cg:, near], height - cg, 1)[:, : end - done]
        if gathered:
            s_in[0, :, done:end] = total.astype(BF16)
        else:
            at = slice(done, min(s_send.shape[2], -(-end // LANES) * LANES))
            for k in range(members):
                s_send[k, :, done:end] = total[rows * k : rows * (k + 1)].astype(BF16)
            for k in range(members):
                push(
                    s_send.at[k, :, pl.ds(at.start, at.stop - at.start)],
                    s_in.at[chunk_of, :, pl.ds(at.start, at.stop - at.start)], 7, 9, group * members + k,
                )
        done = end

    for k in range(2, steps):
        send_outputs(k)

    edges_arrived(cot_left, cot_right, 6, 7)
    for b in range(2):
        edge = lane_contract(
            eye[:cg, :cg],
            jnp.concatenate(
                [
                    jnp.where(has_right > 0, cot_right[8 * b : 8 * (b + 1)].astype(F32), 0.0),
                    jnp.zeros((LANES - 16, cg), F32),
                    jnp.where(has_left > 0, cot_left[8 * b : 8 * (b + 1)].astype(F32), 0.0),
                ],
                axis=0,
            ).astype(BF16),
        ).astype(BF16)
        line = jnp.concatenate(
            [cot_in[:, band * k + half * b : band * k + half * (b + 1)] for k in range(GROUPS)] + [edge], axis=1
        )
        for s in range(-2, 3):
            top = cg * (2 * (s + 2) + b)
            cot_unf[top : top + cg, :] = (line if s == 0 else pltpu.roll(line, (-s) % width, 1))[:, :q]

    def backward(i, total):
        cols = pl.ds(pl.multiple_of(i * 256, 256), 256)
        grad = dot(lhs_grad[...], cot_unf[:, cols])
        pre_grad = (grad * slope[:, cols]).astype(BF16)
        return (
            total
            + lane_contract(pre_grad[:pair], onehot[0, :, cols])
            + lane_contract(pre_grad[pair:], onehot[1, :, cols])
        )

    terms = lax.fori_loop(0, q // 256, backward, jnp.zeros((pair, 8 * SPAN), F32), unroll=True)
    shifted = jnp.concatenate([terms[cg:], jnp.zeros((cg, LANES - 8 * SPAN), F32)], axis=1)
    terms = terms[:cg, : 8 * TAPS] + pltpu.roll(shifted, LANES - 8, 1)[:, : 8 * TAPS]
    if gathered:
        t_in[0, :, : 8 * TAPS] = terms
    else:
        for k in range(members):
            t_send[k, :, : 8 * TAPS] = terms[rows * k : rows * (k + 1)]
        for k in range(members):
            push(t_send.at[k], t_in.at[chunk_of], 8, 10, group * members + k)

    arrived(comb_in, 8)
    for j in range(channels // band):
        part = comb_in[...].reshape(channels, band)[band * j : band * (j + 1)]
        gather = (iota((band, band), 1) == (iota((band, band), 0) % 2) * half + iota((band, band), 0) // 2)
        comb_out[:, band * j : band * (j + 1)] = lane_contract(gather.astype(F32).astype(BF16), part).astype(BF16)
    if not gathered:
        arrived(s_in, 9)
    second_out[...] = jnp.sum(s_in[:, :, :taps].astype(F32), axis=0)
    if not gathered:
        arrived(t_in, 10)
    first_out[...] = dot(split_halves(jnp.sum(t_in[:, :, : 8 * TAPS], axis=0)), diag_ref[...])

    for remote, away in started:
        if away is None:
            remote.wait_send()
            continue

        @pl.when(away)
        def _():
            remote.wait_send()


def finish_kernel(*refs):
    sems = refs[6]
    copies = [pltpu.make_async_copy(refs[k], refs[3 + k], sems.at[k]) for k in range(3)]
    for copy in copies:
        copy.start()
    for copy in copies:
        copy.wait()


def per_device(bases, base_table, first_kernel, second_kernel, cotangent):
    band, channels = cotangent.shape
    cg = channels // GROUPS
    count = lax.axis_size("seq")
    members = count // GROUPS
    rows = first_kernel.shape[0]
    gathered = rows % 16 != 0
    half = band // 2
    q = half * GROUPS
    width = q + LANES
    pair = 2 * cg
    taps = TAPS * cg
    span = SPAN * cg
    deep = 2 * (span + 64)

    lot = 1 if gathered else members
    if gathered:
        group = group_of(lax.axis_index("seq") % GROUPS)
        first_kernel, second_kernel = (
            lax.dynamic_slice_in_dim(lax.all_gather(k, "seq", axis=0, tiled=True), group * cg, cg, 0)
            for k in (first_kernel, second_kernel)
        )
        rows = cg

    vmem = pltpu.VMEM
    outs = pl.pallas_call(
        functools.partial(block_kernel, count, members, gathered),
        out_shape=(
            vmem((band, channels), BF16),
            vmem((rows, taps), F32),
            vmem((rows, taps), F32),
        ),
        in_specs=[pl.BlockSpec(memory_space=pl.ANY)] * 5,
        out_specs=[pl.BlockSpec(memory_space=vmem)] * 3,
        scratch_shapes=[
            vmem((1, band), jnp.int32),
            vmem(base_table.shape, BF16),
            vmem(first_kernel.shape, BF16),
            vmem(second_kernel.shape, BF16),
            vmem((band, channels), BF16),
            vmem((8 * TAPS, taps), BF16),
            vmem((cg, 16), BF16),
            vmem((1, band), F32),
            vmem((band, channels), BF16),
            vmem((channels, band), BF16),
            vmem((2, GROUPS, 16, cg), BF16),
            vmem((1, 2 * q), F32),
            vmem((1, band), F32),
            vmem((1, band), F32),
            vmem((rows, LANES), BF16),
            vmem((lot, rows, LANES), BF16),
            vmem((lot, rows, taps), BF16),
            vmem((cg, 2 * q), BF16),
            vmem((16, cg), BF16),
            vmem((16, cg), BF16),
            vmem((cg, 2 * q), BF16),
            vmem((GROUPS, cg, band), BF16),
            vmem((lot, rows, -(-taps // LANES) * LANES), BF16),
            vmem((lot, rows, -(-taps // LANES) * LANES), BF16),
            vmem((lot, rows, LANES), F32),
            vmem((lot, rows, LANES), F32),
            vmem((2, 8 * SPAN, width), BF16),
            vmem((2, 2 * LANES, width), BF16),
            vmem((2 * pair, q), F32),
            vmem((deep, q), BF16),
            vmem((span, q), BF16),
            vmem((pair, span + 64), F32),
            vmem((pair, deep), BF16),
            vmem((2 * pair, span), BF16),
            pltpu.SemaphoreType.DMA((9,)),
            pltpu.SemaphoreType.DMA((11,)),
            pltpu.SemaphoreType.DMA((5,)),
        ],
        compiler_params=pltpu.CompilerParams(
            collective_id=0, has_side_effects=True, vmem_limit_bytes=56 * 1024 * 1024
        ),
    )(bases.reshape(1, band), base_table, first_kernel, second_kernel, cotangent)

    outs = pl.pallas_call(
        finish_kernel,
        out_shape=tuple(jax.ShapeDtypeStruct(o.shape, o.dtype) for o in outs),
        in_specs=[pl.BlockSpec(memory_space=vmem)] * 3,
        out_specs=[pl.BlockSpec(memory_space=pl.ANY)] * 3,
        scratch_shapes=[pltpu.SemaphoreType.DMA((3,))],
    )(*[pltpu.with_memory_space_constraint(o, vmem) for o in outs])
    if gathered:
        def scatter(part):
            whole = lax.dynamic_update_slice_in_dim(jnp.zeros((channels, taps), F32), part, group * cg, 0)
            return lax.psum_scatter(whole, "seq", scatter_dimension=0, tiled=True)

        return outs[0], scatter(outs[1]), scatter(outs[2])
    return tuple(outs)


def solution(mesh):
    return jax.shard_map(
        per_device,
        mesh=mesh,
        in_specs=(
            P(("groups", "seq")),
            P(),
            P("seq", None),
            P("seq", None),
            P(("groups", "seq"), None),
        ),
        out_specs=(
            P(("groups", "seq"), None),
            P(("groups", "seq"), None),
            P(("groups", "seq"), None),
        ),
        check_vma=False,
    )
```

```python
import functools
import math

import jax
import jax.numpy as jnp
from jax import lax
from jax.experimental import pallas as pl
from jax.experimental.pallas import tpu as pltpu
from jax.sharding import PartitionSpec as P

GROUPS = 8
TAPS = 9
HALF = TAPS // 2
SPAN = TAPS + 1
LANES = 128
MESH = pl.DeviceIdType.MESH
F32 = jnp.float32
BF16 = jnp.bfloat16


def lane_contract(left, right):
    return lax.dot_general(left, right, (((1,), (1,)), ((), ())), preferred_element_type=F32)


def dot(left, right):
    return jnp.dot(left, right, preferred_element_type=F32)


def iota(shape, axis):
    return lax.broadcasted_iota(jnp.int32, shape, axis)


def split_halves(values):
    high = values.astype(BF16).astype(F32)
    return jnp.where((iota(values.shape, 1) & 7) < 4, high, values - high).astype(BF16)


def group_of(place):
    return place // 2 + (GROUPS // 2) * (place % 2)


def place_of(group):
    return (group % (GROUPS // 2)) * 2 + group // (GROUPS // 2)


def gelu_and_slope(pre):
    z = jnp.abs(pre) * math.sqrt(0.5)
    t = pl.reciprocal(1.0 + 0.3275911 * z)
    e = jnp.exp(-0.5 * pre * pre)
    series = 1.061405429
    for c in (-1.453152027, 1.421413741, -0.284496736, 0.254829592):
        series = series * t + c
    tail = (0.5 * series) * (t * e)
    cdf = jnp.where(pre < 0, tail, 1.0 - tail)
    return pre * cdf, cdf + pre * (e * (1.0 / math.sqrt(2.0 * math.pi)))


def block_kernel(
    count, members, gathered,
    bases_hbm, table_hbm, first_hbm, second_hbm, cot_hbm,
    comb_out, first_out, second_out,
    bases_ref, table_ref, first_ref, second_ref, cot_ref,
    diag_ref, skip_ref, codes_ref, cot_perm, cot_t, edges,
    codes_in, codes_left, codes_right, mix_send, mix_in, second_in,
    cot_in, cot_left, cot_right, comb_send, comb_in, s_send, s_in, t_send, t_in,
    onehot, hid, slope, unf, cot_unf, r_acc, lhs_out, lhs_grad,
    send_sems, recv_sems, load_sems,
):
    me = lax.axis_index("seq")
    chunk_of = me // GROUPS
    place = me % GROUPS
    group = group_of(place)
    chunks = count // GROUPS
    band = cot_ref.shape[0]
    cg = cot_in.shape[0]
    pair = 2 * cg
    taps = TAPS * cg
    span = SPAN * cg
    deep = span + 64
    half = band // 2
    q = half * GROUPS
    width = q + LANES
    channels = GROUPS * cg
    rows = cg if gathered else cg // members
    owner = me // members
    member = me % members
    started = []

    def push(src, dst, kind, recv, target, here=None):
        remote = pltpu.make_async_remote_copy(
            src_ref=src, dst_ref=dst, send_sem=send_sems.at[kind], recv_sem=recv_sems.at[recv],
            device_id={"seq": target}, device_id_type=MESH,
        )
        away = target != me
        if here is not None:
            away = here & away
            local = here & (target == me)
        else:
            local = target == me

        @pl.when(away)
        def _():
            remote.start()

        @pl.when(local)
        def _():
            pltpu.make_async_copy(src, dst, recv_sems.at[recv]).start()

        started.append((remote, away))

    def arrived(ref, recv):
        pltpu.make_async_copy(ref, ref, recv_sems.at[recv]).wait()

    def push_chunk(src_of, dst, kind, recv):
        for k in range(GROUPS):
            to = (place + k + 1) % GROUPS
            push(src_of(to), dst, kind, recv, chunk_of * GROUPS + to)

    def push_edges(src_of, left_dst, right_dst, kind, recv_left, recv_right):
        for low, dst, recv, here, there in (
            (True, right_dst, recv_right, (place == 0) & (chunk_of > 0), chunk_of - 1),
            (False, left_dst, recv_left, (place == GROUPS - 1) & (chunk_of < chunks - 1), chunk_of + 1),
        ):
            for to in range(GROUPS):
                push(src_of(to, low), dst, kind, recv, there * GROUPS + to, here)

    def edges_arrived(left, right, recv_left, recv_right):
        @pl.when(chunk_of > 0)
        def _():
            arrived(left, recv_left)

        @pl.when(chunk_of < chunks - 1)
        def _():
            arrived(right, recv_right)

    barrier = pltpu.get_barrier_semaphore()
    for k in range(1, count):
        pl.semaphore_signal(barrier, inc=1, device_id={"seq": (me + k) % count}, device_id_type=MESH)

    loads = [
        pltpu.make_async_copy(src, dst, load_sems.at[k])
        for k, (src, dst) in enumerate(
            (
                (bases_hbm, bases_ref), (table_hbm, table_ref), (first_hbm, first_ref),
                (cot_hbm, cot_ref), (second_hbm, second_ref),
            )
        )
    ]
    for load in loads:
        load.start()

    spread = (iota((band, band), 1) == 2 * (iota((band, band), 0) % half) + iota((band, band), 0) // half)
    spread = spread.astype(F32).astype(BF16)
    loads[0].wait()
    bases = jnp.broadcast_to(bases_ref[...], (8, band)).astype(F32).astype(BF16)
    codes = lane_contract(bases, spread)
    codes_ref[...] = codes[0:1]

    loads[1].wait()
    table = table_ref[...].astype(F32)
    code = iota((8, channels), 0)
    wide = jnp.zeros((8, channels), F32)
    turned = jnp.zeros((8, channels), F32)
    for c in range(4):
        wide = jnp.where(code % 4 == c, table[c : c + 1], wide)
        turned = jnp.where(code == 7 - c, table[c : c + 1], turned)
    lane = iota((8, channels), 1)
    whose = group if gathered else owner
    strand = jnp.where(lane < cg, pltpu.roll(wide, (channels - whose * cg) % channels, 1), 0.0)
    strand = jnp.concatenate([strand, jnp.zeros((8, LANES), F32)], axis=1)
    diag_ref[...] = jnp.concatenate([pltpu.roll(strand, cg * t, 1) for t in range(TAPS)], axis=0)[:, :taps].astype(BF16)
    own = pltpu.roll(jnp.where(code < 4, wide, turned), (channels - group * cg) % channels, 1)[:, :cg]
    eye = (iota((band, band), 0) == iota((band, band), 1)).astype(F32).astype(BF16)
    skip_ref[...] = lane_contract(
        eye[:cg, :cg],
        jnp.concatenate([own, jnp.zeros((8, cg), F32)], axis=0).astype(BF16),
    ).astype(BF16)
    loads[2].wait()
    mix = split_halves(lane_contract(first_ref[...], diag_ref[...]))
    if gathered:
        mix_in[0, :, : 8 * TAPS] = mix
    else:
        mix_send[:, : 8 * TAPS] = mix

    loads[3].wait()
    for j in range(channels // band):
        cot_perm[:, band * j : band * (j + 1)] = dot(
            spread, cot_ref[:, band * j : band * (j + 1)]
        ).astype(BF16)
    for j in range(channels // band):
        cot_t[band * j : band * (j + 1)] = lane_contract(
            eye, cot_perm[:, band * j : band * (j + 1)]
        ).astype(BF16)
    for to in range(GROUPS):
        g = group_of(to)
        lanes = slice(cg * g, cg * (g + 1))
        edges[0, to] = jnp.concatenate([cot_perm[half * b : half * b + 8, lanes] for b in range(2)], axis=0)
        edges[1, to] = jnp.concatenate([cot_perm[half * (b + 1) - 8 : half * (b + 1), lanes] for b in range(2)], axis=0)

    loads[4].wait()
    pl.semaphore_wait(barrier, count - 1)

    here = pl.ds(pl.multiple_of(place * band, LANES), band)
    push_chunk(lambda to: codes_ref, codes_in.at[:, here], 0, 0)
    push_edges(lambda to, low: codes_ref, codes_left, codes_right, 1, 1, 2)
    if not gathered:
        for c in range(chunks):
            push(mix_send, mix_in.at[member], 2, 3, c * GROUPS + place_of(owner))
    if not gathered:
        for c in range(1, chunks + 1):
            push(second_ref, second_in.at[member], 3, 4, (chunk_of + c) % chunks * GROUPS + place_of(owner))
    here = pl.ds(pl.multiple_of(place * band, LANES), band)
    push_chunk(
        lambda to: cot_t.at[pl.ds(pl.multiple_of(group_of(to) * cg, 16), cg)], cot_in.at[:, here], 4, 5
    )
    push_edges(lambda to, low: edges.at[0 if low else 1, to], cot_left, cot_right, 5, 6, 7)

    has_right = (chunk_of < chunks - 1).astype(jnp.int32)
    has_left = (chunk_of > 0).astype(jnp.int32)

    def edge_mask(height):
        lane = iota((height, LANES), 1)
        return lane < LANES // 2, jnp.where(lane < LANES // 2, has_right, has_left) > 0

    for a in range(2):
        for s in range(2):
            hid[a, LANES * s + cg : LANES * (s + 1), :] = jnp.zeros((LANES - cg, width), BF16)
    arrived(codes_in, 0)
    edges_arrived(codes_left, codes_right, 1, 2)
    on_right, real = edge_mask(1)
    lines = []
    for b in range(2):
        edge = jnp.where(on_right, codes_right[:, half * b : half * b + LANES], codes_left[:, half * (b + 1) - LANES : half * (b + 1)])
        line = [codes_in[:, band * k + half * b : band * k + half * (b + 1)] for k in range(GROUPS)]
        lines.append(jnp.broadcast_to(jnp.concatenate(line + [jnp.where(real, edge, 4.0)], axis=1), (8, width)))
    want = (iota((8, width), 0) & 3).astype(F32)
    moved = {}
    for b in range(2):
        for s in range(-2, 3):
            moved[s, b] = lines[b] if s == 0 else pltpu.roll(lines[b], (-s) % width, 1)
    for strand in range(2):
        blocks = []
        for j in range(SPAN):
            value = moved[j // 2 - 2, j % 2] if strand == 0 else 3.0 - moved[2 - j // 2, 1 - j % 2]
            blocks.append(jnp.where(value == want, 1.0, 0.0))
        onehot[strand] = jnp.concatenate(blocks, axis=0).astype(BF16)
    for strand in range(2):
        top = strand * deep + span
        unf[top : top + 16, :] = onehot[0, 8 * HALF : 8 * HALF + 16, :q]

    if not gathered:
        arrived(mix_in, 3)
    mix = mix_in[...].reshape(cg, LANES).astype(F32)
    mix = jnp.where(iota((cg, LANES), 1) < 8 * TAPS, mix, 0.0)
    mix = jnp.concatenate([mix, pltpu.roll(mix, 8, 1)], axis=0)[:, : 8 * SPAN].astype(BF16)

    def store_hidden(strand, cols, hidden):
        for k in range(2):
            hid[k if strand == 0 else 1 - k, LANES * strand : LANES * strand + cg, cols] = hidden[cg * k : cg * (k + 1)]

    def activate(cols):
        for strand in range(2):
            hidden, grad = gelu_and_slope(dot(mix, onehot[strand, :, cols]))
            store_hidden(strand, cols, hidden.astype(BF16))
            slope[pair * strand : pair * (strand + 1), cols] = grad

    def unfold(i):
        for b in range(2):
            for strand in range(2):
                rows_at = slice(LANES * strand, LANES * strand + cg)
                low = 256 * i - LANES
                if low < 0:
                    line = jnp.concatenate([hid[b, rows_at, q:], hid[b, rows_at, : 256 + LANES]], axis=1)
                else:
                    line = hid[b, rows_at, low : low + 512]
                for s in range(-2, 3):
                    j = 2 * (s + 2) + b if strand == 0 else 2 * (2 - s) + 1 - b
                    top = strand * deep + cg * j
                    moved = line if s == 0 else pltpu.roll(line, (-s) % 512, 1)
                    unf[top : top + cg, 256 * i : 256 * (i + 1)] = moved[:, LANES : LANES + 256]

    _, real = edge_mask(pair)
    for strand in range(2):
        hidden, _ = gelu_and_slope(dot(mix, onehot[strand, :, q:]))
        store_hidden(strand, slice(q, width), jnp.where(real, hidden, 0.0).astype(BF16))
    blocks = q // 256
    for i in range(blocks):
        activate(slice(256 * i, 256 * (i + 1)))
        if i > 0:
            unfold(i - 1)
    unfold(blocks - 1)

    if gathered:
        second = second_ref[...]
    else:
        arrived(second_in, 4)
        second = second_in[...].reshape(cg, taps)
    own = jnp.concatenate([skip_ref[...], jnp.zeros((cg, LANES - 16), BF16)], axis=1).astype(F32)
    part = jnp.concatenate([second, jnp.zeros((cg, deep - taps), BF16)], axis=1).astype(F32)
    lag = pltpu.roll(part, cg, 1)
    for strand in range(2):
        x = jnp.where(iota((cg, LANES), 1) // 4 == strand, own, 0.0)
        x = jnp.concatenate([jnp.zeros((cg, deep - LANES), F32), pltpu.roll(x, LANES // 2, 1)], axis=1)
        at = slice(deep * strand, deep * (strand + 1))
        lhs_out[0:cg, at] = ((part, lag)[strand] + x).astype(BF16)
        lhs_out[cg:, at] = ((lag, part)[strand] + pltpu.roll(x, 8, 1)).astype(BF16)

    steps = GROUPS // 2

    def send_outputs(k):
        pick = (place // 2 + 1 + k) % steps
        cols = pl.ds(pl.multiple_of(pick * band, LANES), band)
        out, back = (
            dot(lhs_out[:, deep * strand : deep * strand + span + 16], unf[deep * strand : deep * strand + span + 16, cols])
            for strand in range(2)
        )
        out = (out + back.astype(BF16).astype(F32)).astype(BF16)
        comb_send[:, pl.ds(pl.multiple_of(2 * pick * band, LANES), 2 * band)] = jnp.concatenate(
            [out[cg * a : cg * (a + 1), half * b : half * (b + 1)] for b in range(2) for a in range(2)], axis=1
        )
        for b in range(2):
            side = (place + 1 + b) % 2
            at = pl.ds(pl.multiple_of((2 * pick + side) * band, LANES), band)
            if k == steps - 1 and b == 1:
                pltpu.make_async_copy(comb_send.at[:, at], comb_in.at[group], recv_sems.at[8]).start()
            else:
                remote = pltpu.make_async_remote_copy(
                    src_ref=comb_send.at[:, at], dst_ref=comb_in.at[group], send_sem=send_sems.at[6],
                    recv_sem=recv_sems.at[8], device_id={"seq": chunk_of * GROUPS + 2 * pick + side},
                    device_id_type=MESH,
                )
                remote.start()
                started.append((remote, None))

    for k in range(2):
        send_outputs(k)

    stack = []
    for t in range(SPAN):
        lowered = second[:, cg * (8 - t) : cg * (9 - t)] if t < TAPS else jnp.zeros((cg, cg), BF16)
        raised = second[:, cg * (9 - t) : cg * (10 - t)] if t > 0 else jnp.zeros((cg, cg), BF16)
        before = second[:, cg * (t - 1) : cg * t] if t > 0 else jnp.zeros((cg, cg), BF16)
        after = second[:, cg * t : cg * (t + 1)] if t < TAPS else jnp.zeros((cg, cg), BF16)
        stack.append(jnp.concatenate([lowered, raised, before, after], axis=1))
    stack = jnp.concatenate(stack, axis=0)
    for strand in range(2):
        lhs_grad[pair * strand : pair * (strand + 1)] = lane_contract(
            eye[:pair, :pair], stack[:, pair * strand : pair * (strand + 1)]
        ).astype(BF16)

    arrived(cot_in, 5)
    even, odd = (
        jnp.concatenate([cot_in[:, band * k + half * b : band * k + half * (b + 1)] for k in range(GROUPS)], axis=1)
        for b in range(2)
    )
    forward = jnp.concatenate([even, odd], axis=0)
    reverse = jnp.concatenate([odd, even], axis=0)
    parts = (0, 512, span)
    done = 0
    for low, high in zip(parts[:-1], parts[1:]):
        for n in range(low, high, 256):
            size = min(256, high - n)
            r_acc[:, n : n + size] = lane_contract(forward, unf[n : n + size, :]) + lane_contract(
                reverse, unf[deep + n : deep + n + size, :]
            )
        end = taps if high == span else (high - cg) // LANES * LANES
        near = slice(done, min(r_acc.shape[1], -(-(end + cg) // LANES) * LANES))
        height = near.stop - near.start
        total = r_acc[0:cg, done:end] + pltpu.roll(r_acc[cg:, near], height - cg, 1)[:, : end - done]
        if gathered:
            s_in[0, :, done:end] = total.astype(BF16)
        else:
            at = slice(done, min(s_send.shape[2], -(-end // LANES) * LANES))
            for k in range(members):
                s_send[k, :, done:end] = total[rows * k : rows * (k + 1)].astype(BF16)
            for k in range(members):
                push(
                    s_send.at[k, :, pl.ds(at.start, at.stop - at.start)],
                    s_in.at[chunk_of, :, pl.ds(at.start, at.stop - at.start)], 7, 9, group * members + k,
                )
        done = end

    for k in range(2, steps):
        send_outputs(k)

    edges_arrived(cot_left, cot_right, 6, 7)
    for b in range(2):
        edge = lane_contract(
            eye[:cg, :cg],
            jnp.concatenate(
                [
                    jnp.where(has_right > 0, cot_right[8 * b : 8 * (b + 1)].astype(F32), 0.0),
                    jnp.zeros((LANES - 16, cg), F32),
                    jnp.where(has_left > 0, cot_left[8 * b : 8 * (b + 1)].astype(F32), 0.0),
                ],
                axis=0,
            ).astype(BF16),
        ).astype(BF16)
        line = jnp.concatenate(
            [cot_in[:, band * k + half * b : band * k + half * (b + 1)] for k in range(GROUPS)] + [edge], axis=1
        )
        for s in range(-2, 3):
            top = cg * (2 * (s + 2) + b)
            cot_unf[top : top + cg, :] = (line if s == 0 else pltpu.roll(line, (-s) % width, 1))[:, :q]

    def backward(i, total):
        cols = pl.ds(pl.multiple_of(i * 256, 256), 256)
        grad = dot(lhs_grad[...], cot_unf[:, cols])
        pre_grad = (grad * slope[:, cols]).astype(BF16)
        return (
            total
            + lane_contract(pre_grad[:pair], onehot[0, :, cols])
            + lane_contract(pre_grad[pair:], onehot[1, :, cols])
        )

    terms = lax.fori_loop(0, q // 256, backward, jnp.zeros((pair, 8 * SPAN), F32), unroll=True)
    shifted = jnp.concatenate([terms[cg:], jnp.zeros((cg, LANES - 8 * SPAN), F32)], axis=1)
    terms = terms[:cg, : 8 * TAPS] + pltpu.roll(shifted, LANES - 8, 1)[:, : 8 * TAPS]
    if gathered:
        t_in[0, :, : 8 * TAPS] = terms
    else:
        for k in range(members):
            t_send[k, :, : 8 * TAPS] = terms[rows * k : rows * (k + 1)]
        for k in range(members):
            push(t_send.at[k], t_in.at[chunk_of], 8, 10, group * members + k)

    arrived(comb_in, 8)
    for j in range(channels // band):
        part = comb_in[...].reshape(channels, band)[band * j : band * (j + 1)]
        gather = (iota((band, band), 1) == (iota((band, band), 0) % 2) * half + iota((band, band), 0) // 2)
        comb_out[:, band * j : band * (j + 1)] = lane_contract(gather.astype(F32).astype(BF16), part).astype(BF16)
    if not gathered:
        arrived(s_in, 9)
    second_out[...] = jnp.sum(s_in[:, :, :taps].astype(F32), axis=0)
    if not gathered:
        arrived(t_in, 10)
    first_out[...] = dot(split_halves(jnp.sum(t_in[:, :, : 8 * TAPS], axis=0)), diag_ref[...])

    for remote, away in started:
        if away is None:
            remote.wait_send()
            continue

        @pl.when(away)
        def _():
            remote.wait_send()


def finish_kernel(*refs):
    sems = refs[6]
    copies = [pltpu.make_async_copy(refs[k], refs[3 + k], sems.at[k]) for k in range(3)]
    for copy in copies:
        copy.start()
    for copy in copies:
        copy.wait()


def per_device(bases, base_table, first_kernel, second_kernel, cotangent):
    band, channels = cotangent.shape
    cg = channels // GROUPS
    count = lax.axis_size("seq")
    members = count // GROUPS
    rows = first_kernel.shape[0]
    gathered = rows % 16 != 0
    half = band // 2
    q = half * GROUPS
    width = q + LANES
    pair = 2 * cg
    taps = TAPS * cg
    span = SPAN * cg
    deep = 2 * (span + 64)

    lot = 1 if gathered else members
    if gathered:
        group = group_of(lax.axis_index("seq") % GROUPS)
        first_kernel, second_kernel = (
            lax.dynamic_slice_in_dim(lax.all_gather(k, "seq", axis=0, tiled=True), group * cg, cg, 0)
            for k in (first_kernel, second_kernel)
        )
        rows = cg

    vmem = pltpu.VMEM
    outs = pl.pallas_call(
        functools.partial(block_kernel, count, members, gathered),
        out_shape=(
            vmem((band, channels), BF16),
            vmem((rows, taps), F32),
            vmem((rows, taps), F32),
        ),
        in_specs=[pl.BlockSpec(memory_space=pl.ANY)] * 5,
        out_specs=[pl.BlockSpec(memory_space=vmem)] * 3,
        scratch_shapes=[
            vmem((1, band), jnp.int32),
            vmem(base_table.shape, BF16),
            vmem(first_kernel.shape, BF16),
            vmem(second_kernel.shape, BF16),
            vmem((band, channels), BF16),
            vmem((8 * TAPS, taps), BF16),
            vmem((cg, 16), BF16),
            vmem((1, band), F32),
            vmem((band, channels), BF16),
            vmem((channels, band), BF16),
            vmem((2, GROUPS, 16, cg), BF16),
            vmem((1, 2 * q), F32),
            vmem((1, band), F32),
            vmem((1, band), F32),
            vmem((rows, LANES), BF16),
            vmem((lot, rows, LANES), BF16),
            vmem((lot, rows, taps), BF16),
            vmem((cg, 2 * q), BF16),
            vmem((16, cg), BF16),
            vmem((16, cg), BF16),
            vmem((cg, 2 * q), BF16),
            vmem((GROUPS, cg, band), BF16),
            vmem((lot, rows, -(-taps // LANES) * LANES), BF16),
            vmem((lot, rows, -(-taps // LANES) * LANES), BF16),
            vmem((lot, rows, LANES), F32),
            vmem((lot, rows, LANES), F32),
            vmem((2, 8 * SPAN, width), BF16),
            vmem((2, 2 * LANES, width), BF16),
            vmem((2 * pair, q), F32),
            vmem((deep, q), BF16),
            vmem((span, q), BF16),
            vmem((pair, span + 64), F32),
            vmem((pair, deep), BF16),
            vmem((2 * pair, span), BF16),
            pltpu.SemaphoreType.DMA((9,)),
            pltpu.SemaphoreType.DMA((11,)),
            pltpu.SemaphoreType.DMA((5,)),
        ],
        compiler_params=pltpu.CompilerParams(
            collective_id=0, has_side_effects=True, vmem_limit_bytes=56 * 1024 * 1024
        ),
    )(bases.reshape(1, band), base_table, first_kernel, second_kernel, cotangent)

    outs = pl.pallas_call(
        finish_kernel,
        out_shape=tuple(jax.ShapeDtypeStruct(o.shape, o.dtype) for o in outs),
        in_specs=[pl.BlockSpec(memory_space=vmem)] * 3,
        out_specs=[pl.BlockSpec(memory_space=pl.ANY)] * 3,
        scratch_shapes=[pltpu.SemaphoreType.DMA((3,))],
    )(*[pltpu.with_memory_space_constraint(o, vmem) for o in outs])
    if gathered:
        def scatter(part):
            whole = lax.dynamic_update_slice_in_dim(jnp.zeros((channels, taps), F32), part, group * cg, 0)
            return lax.psum_scatter(whole, "seq", scatter_dimension=0, tiled=True)

        return outs[0], scatter(outs[1]), scatter(outs[2])
    return tuple(outs)


def solution(mesh):
    return jax.shard_map(
        per_device,
        mesh=mesh,
        in_specs=(
            P(("groups", "seq")),
            P(),
            P("seq", None),
            P("seq", None),
            P(("groups", "seq"), None),
        ),
        out_specs=(
            P(("groups", "seq"), None),
            P(("groups", "seq"), None),
            P(("groups", "seq"), None),
        ),
        check_vma=False,
    )
```

```python
import functools
import math

import jax
import jax.numpy as jnp
from jax import lax
from jax.experimental import pallas as pl
from jax.experimental.pallas import tpu as pltpu
from jax.sharding import PartitionSpec as P

GROUPS = 8
TAPS = 9
HALF = TAPS // 2
SPAN = TAPS + 1
LANES = 128
MESH = pl.DeviceIdType.MESH
F32 = jnp.float32
BF16 = jnp.bfloat16


def lane_contract(left, right):
    return lax.dot_general(left, right, (((1,), (1,)), ((), ())), preferred_element_type=F32)


def dot(left, right):
    return jnp.dot(left, right, preferred_element_type=F32)


def iota(shape, axis):
    return lax.broadcasted_iota(jnp.int32, shape, axis)


def split_halves(values):
    high = values.astype(BF16).astype(F32)
    return jnp.where((iota(values.shape, 1) & 7) < 4, high, values - high).astype(BF16)


def group_of(place):
    return place // 2 + (GROUPS // 2) * (place % 2)


def place_of(group):
    return (group % (GROUPS // 2)) * 2 + group // (GROUPS // 2)


def gelu_and_slope(pre):
    z = jnp.abs(pre) * math.sqrt(0.5)
    t = pl.reciprocal(1.0 + 0.3275911 * z)
    e = jnp.exp(-0.5 * pre * pre)
    series = 1.061405429
    for c in (-1.453152027, 1.421413741, -0.284496736, 0.254829592):
        series = series * t + c
    tail = (0.5 * series) * (t * e)
    cdf = jnp.where(pre < 0, tail, 1.0 - tail)
    return pre * cdf, cdf + pre * (e * (1.0 / math.sqrt(2.0 * math.pi)))


def block_kernel(
    count, members, gathered,
    bases_hbm, table_hbm, first_hbm, second_hbm, cot_hbm,
    comb_out, first_out, second_out,
    bases_ref, table_ref, first_ref, second_ref, cot_ref,
    diag_ref, skip_ref, codes_ref, cot_perm, cot_t, edges,
    codes_in, codes_left, codes_right, mix_send, mix_in, second_in,
    cot_in, cot_left, cot_right, comb_send, comb_in, s_send, s_in, t_send, t_in,
    onehot, hid, slope, unf, cot_unf, r_acc, lhs_out, lhs_grad,
    send_sems, recv_sems, load_sems,
):
    me = lax.axis_index("seq")
    chunk_of = me // GROUPS
    place = me % GROUPS
    group = group_of(place)
    chunks = count // GROUPS
    band = cot_ref.shape[0]
    cg = cot_in.shape[0]
    pair = 2 * cg
    taps = TAPS * cg
    span = SPAN * cg
    deep = span + 64
    half = band // 2
    q = half * GROUPS
    width = q + LANES
    channels = GROUPS * cg
    rows = cg if gathered else cg // members
    owner = me // members
    member = me % members
    started = []

    def push(src, dst, kind, recv, target, here=None):
        remote = pltpu.make_async_remote_copy(
            src_ref=src, dst_ref=dst, send_sem=send_sems.at[kind], recv_sem=recv_sems.at[recv],
            device_id={"seq": target}, device_id_type=MESH,
        )
        away = target != me
        if here is not None:
            away = here & away
            local = here & (target == me)
        else:
            local = target == me

        @pl.when(away)
        def _():
            remote.start()

        @pl.when(local)
        def _():
            pltpu.make_async_copy(src, dst, recv_sems.at[recv]).start()

        started.append((remote, away))

    def arrived(ref, recv):
        pltpu.make_async_copy(ref, ref, recv_sems.at[recv]).wait()

    def push_chunk(src_of, dst, kind, recv):
        for k in range(GROUPS):
            to = (place + k + 1) % GROUPS
            push(src_of(to), dst, kind, recv, chunk_of * GROUPS + to)

    def push_edges(src_of, left_dst, right_dst, kind, recv_left, recv_right):
        for low, dst, recv, here, there in (
            (True, right_dst, recv_right, (place == 0) & (chunk_of > 0), chunk_of - 1),
            (False, left_dst, recv_left, (place == GROUPS - 1) & (chunk_of < chunks - 1), chunk_of + 1),
        ):
            for to in range(GROUPS):
                push(src_of(to, low), dst, kind, recv, there * GROUPS + to, here)

    def edges_arrived(left, right, recv_left, recv_right):
        @pl.when(chunk_of > 0)
        def _():
            arrived(left, recv_left)

        @pl.when(chunk_of < chunks - 1)
        def _():
            arrived(right, recv_right)

    barrier = pltpu.get_barrier_semaphore()
    for k in range(1, count):
        pl.semaphore_signal(barrier, inc=1, device_id={"seq": (me + k) % count}, device_id_type=MESH)

    loads = [
        pltpu.make_async_copy(src, dst, load_sems.at[k])
        for k, (src, dst) in enumerate(
            (
                (bases_hbm, bases_ref), (table_hbm, table_ref), (first_hbm, first_ref),
                (cot_hbm, cot_ref), (second_hbm, second_ref),
            )
        )
    ]
    for load in loads:
        load.start()

    spread = (iota((band, band), 1) == 2 * (iota((band, band), 0) % half) + iota((band, band), 0) // half)
    spread = spread.astype(F32).astype(BF16)
    loads[0].wait()
    bases = jnp.broadcast_to(bases_ref[...], (8, band)).astype(F32).astype(BF16)
    codes = lane_contract(bases, spread)
    codes_ref[...] = codes[0:1]

    loads[1].wait()
    table = table_ref[...].astype(F32)
    code = iota((8, channels), 0)
    wide = jnp.zeros((8, channels), F32)
    turned = jnp.zeros((8, channels), F32)
    for c in range(4):
        wide = jnp.where(code % 4 == c, table[c : c + 1], wide)
        turned = jnp.where(code == 7 - c, table[c : c + 1], turned)
    lane = iota((8, channels), 1)
    whose = group if gathered else owner
    strand = jnp.where(lane < cg, pltpu.roll(wide, (channels - whose * cg) % channels, 1), 0.0)
    strand = jnp.concatenate([strand, jnp.zeros((8, LANES), F32)], axis=1)
    diag_ref[...] = jnp.concatenate([pltpu.roll(strand, cg * t, 1) for t in range(TAPS)], axis=0)[:, :taps].astype(BF16)
    own = pltpu.roll(jnp.where(code < 4, wide, turned), (channels - group * cg) % channels, 1)[:, :cg]
    eye = (iota((band, band), 0) == iota((band, band), 1)).astype(F32).astype(BF16)
    skip_ref[...] = lane_contract(
        eye[:cg, :cg],
        jnp.concatenate([own, jnp.zeros((8, cg), F32)], axis=0).astype(BF16),
    ).astype(BF16)
    loads[2].wait()
    mix = split_halves(lane_contract(first_ref[...], diag_ref[...]))
    if gathered:
        mix_in[0, :, : 8 * TAPS] = mix
    else:
        mix_send[:, : 8 * TAPS] = mix

    loads[3].wait()
    for j in range(channels // band):
        cot_perm[:, band * j : band * (j + 1)] = dot(
            spread, cot_ref[:, band * j : band * (j + 1)]
        ).astype(BF16)
    for j in range(channels // band):
        cot_t[band * j : band * (j + 1)] = lane_contract(
            eye, cot_perm[:, band * j : band * (j + 1)]
        ).astype(BF16)
    for to in range(GROUPS):
        g = group_of(to)
        lanes = slice(cg * g, cg * (g + 1))
        edges[0, to] = jnp.concatenate([cot_perm[half * b : half * b + 8, lanes] for b in range(2)], axis=0)
        edges[1, to] = jnp.concatenate([cot_perm[half * (b + 1) - 8 : half * (b + 1), lanes] for b in range(2)], axis=0)

    loads[4].wait()
    pl.semaphore_wait(barrier, count - 1)

    here = pl.ds(pl.multiple_of(place * band, LANES), band)
    push_chunk(lambda to: codes_ref, codes_in.at[:, here], 0, 0)
    push_edges(lambda to, low: codes_ref, codes_left, codes_right, 1, 1, 2)
    if not gathered:
        for c in range(chunks):
            push(mix_send, mix_in.at[member], 2, 3, c * GROUPS + place_of(owner))
    if not gathered:
        for c in range(1, chunks + 1):
            push(second_ref, second_in.at[member], 3, 4, (chunk_of + c) % chunks * GROUPS + place_of(owner))
    here = pl.ds(pl.multiple_of(place * band, LANES), band)
    push_chunk(
        lambda to: cot_t.at[pl.ds(pl.multiple_of(group_of(to) * cg, 16), cg)], cot_in.at[:, here], 4, 5
    )
    push_edges(lambda to, low: edges.at[0 if low else 1, to], cot_left, cot_right, 5, 6, 7)

    has_right = (chunk_of < chunks - 1).astype(jnp.int32)
    has_left = (chunk_of > 0).astype(jnp.int32)

    def edge_mask(height):
        lane = iota((height, LANES), 1)
        return lane < LANES // 2, jnp.where(lane < LANES // 2, has_right, has_left) > 0

    for a in range(2):
        for s in range(2):
            hid[a, LANES * s + cg : LANES * (s + 1), :] = jnp.zeros((LANES - cg, width), BF16)
    arrived(codes_in, 0)
    edges_arrived(codes_left, codes_right, 1, 2)
    on_right, real = edge_mask(1)
    lines = []
    for b in range(2):
        edge = jnp.where(on_right, codes_right[:, half * b : half * b + LANES], codes_left[:, half * (b + 1) - LANES : half * (b + 1)])
        line = [codes_in[:, band * k + half * b : band * k + half * (b + 1)] for k in range(GROUPS)]
        lines.append(jnp.broadcast_to(jnp.concatenate(line + [jnp.where(real, edge, 4.0)], axis=1), (8, width)))
    want = (iota((8, width), 0) & 3).astype(F32)
    moved = {}
    for b in range(2):
        for s in range(-2, 3):
            moved[s, b] = lines[b] if s == 0 else pltpu.roll(lines[b], (-s) % width, 1)
    for strand in range(2):
        blocks = []
        for j in range(SPAN):
            value = moved[j // 2 - 2, j % 2] if strand == 0 else 3.0 - moved[2 - j // 2, 1 - j % 2]
            blocks.append(jnp.where(value == want, 1.0, 0.0))
        onehot[strand] = jnp.concatenate(blocks, axis=0).astype(BF16)
    for strand in range(2):
        top = strand * deep + span
        unf[top : top + 16, :] = onehot[0, 8 * HALF : 8 * HALF + 16, :q]

    if not gathered:
        arrived(mix_in, 3)
    mix = mix_in[...].reshape(cg, LANES).astype(F32)
    mix = jnp.where(iota((cg, LANES), 1) < 8 * TAPS, mix, 0.0)
    mix = jnp.concatenate([mix, pltpu.roll(mix, 8, 1)], axis=0)[:, : 8 * SPAN].astype(BF16)

    def store_hidden(strand, cols, hidden):
        for k in range(2):
            hid[k if strand == 0 else 1 - k, LANES * strand : LANES * strand + cg, cols] = hidden[cg * k : cg * (k + 1)]

    def activate(cols):
        for strand in range(2):
            hidden, grad = gelu_and_slope(dot(mix, onehot[strand, :, cols]))
            store_hidden(strand, cols, hidden.astype(BF16))
            slope[pair * strand : pair * (strand + 1), cols] = grad

    def unfold(i):
        for b in range(2):
            for strand in range(2):
                rows_at = slice(LANES * strand, LANES * strand + cg)
                low = 256 * i - LANES
                if low < 0:
                    line = jnp.concatenate([hid[b, rows_at, q:], hid[b, rows_at, : 256 + LANES]], axis=1)
                else:
                    line = hid[b, rows_at, low : low + 512]
                for s in range(-2, 3):
                    j = 2 * (s + 2) + b if strand == 0 else 2 * (2 - s) + 1 - b
                    top = strand * deep + cg * j
                    moved = line if s == 0 else pltpu.roll(line, (-s) % 512, 1)
                    unf[top : top + cg, 256 * i : 256 * (i + 1)] = moved[:, LANES : LANES + 256]

    _, real = edge_mask(pair)
    for strand in range(2):
        hidden, _ = gelu_and_slope(dot(mix, onehot[strand, :, q:]))
        store_hidden(strand, slice(q, width), jnp.where(real, hidden, 0.0).astype(BF16))
    blocks = q // 256
    for i in range(blocks):
        activate(slice(256 * i, 256 * (i + 1)))
        if i > 0:
            unfold(i - 1)
    unfold(blocks - 1)

    if gathered:
        second = second_ref[...]
    else:
        arrived(second_in, 4)
        second = second_in[...].reshape(cg, taps)
    own = jnp.concatenate([skip_ref[...], jnp.zeros((cg, LANES - 16), BF16)], axis=1).astype(F32)
    part = jnp.concatenate([second, jnp.zeros((cg, deep - taps), BF16)], axis=1).astype(F32)
    lag = pltpu.roll(part, cg, 1)
    for strand in range(2):
        x = jnp.where(iota((cg, LANES), 1) // 4 == strand, own, 0.0)
        x = jnp.concatenate([jnp.zeros((cg, deep - LANES), F32), pltpu.roll(x, LANES // 2, 1)], axis=1)
        at = slice(deep * strand, deep * (strand + 1))
        lhs_out[0:cg, at] = ((part, lag)[strand] + x).astype(BF16)
        lhs_out[cg:, at] = ((lag, part)[strand] + pltpu.roll(x, 8, 1)).astype(BF16)

    steps = GROUPS // 2

    def send_outputs(k):
        pick = (place // 2 + 1 + k) % steps
        cols = pl.ds(pl.multiple_of(pick * band, LANES), band)
        out, back = (
            dot(lhs_out[:, deep * strand : deep * strand + span + 16], unf[deep * strand : deep * strand + span + 16, cols])
            for strand in range(2)
        )
        out = (out + back.astype(BF16).astype(F32)).astype(BF16)
        comb_send[:, pl.ds(pl.multiple_of(2 * pick * band, LANES), 2 * band)] = jnp.concatenate(
            [out[cg * a : cg * (a + 1), half * b : half * (b + 1)] for b in range(2) for a in range(2)], axis=1
        )
        for b in range(2):
            side = (place + 1 + b) % 2
            at = pl.ds(pl.multiple_of((2 * pick + side) * band, LANES), band)
            if k == steps - 1 and b == 1:
                pltpu.make_async_copy(comb_send.at[:, at], comb_in.at[group], recv_sems.at[8]).start()
            else:
                remote = pltpu.make_async_remote_copy(
                    src_ref=comb_send.at[:, at], dst_ref=comb_in.at[group], send_sem=send_sems.at[6],
                    recv_sem=recv_sems.at[8], device_id={"seq": chunk_of * GROUPS + 2 * pick + side},
                    device_id_type=MESH,
                )
                remote.start()
                started.append((remote, None))

    for k in range(2):
        send_outputs(k)

    stack = []
    for t in range(SPAN):
        lowered = second[:, cg * (8 - t) : cg * (9 - t)] if t < TAPS else jnp.zeros((cg, cg), BF16)
        raised = second[:, cg * (9 - t) : cg * (10 - t)] if t > 0 else jnp.zeros((cg, cg), BF16)
        before = second[:, cg * (t - 1) : cg * t] if t > 0 else jnp.zeros((cg, cg), BF16)
        after = second[:, cg * t : cg * (t + 1)] if t < TAPS else jnp.zeros((cg, cg), BF16)
        stack.append(jnp.concatenate([lowered, raised, before, after], axis=1))
    stack = jnp.concatenate(stack, axis=0)
    for strand in range(2):
        lhs_grad[pair * strand : pair * (strand + 1)] = lane_contract(
            eye[:pair, :pair], stack[:, pair * strand : pair * (strand + 1)]
        ).astype(BF16)

    arrived(cot_in, 5)
    even, odd = (
        jnp.concatenate([cot_in[:, band * k + half * b : band * k + half * (b + 1)] for k in range(GROUPS)], axis=1)
        for b in range(2)
    )
    forward = jnp.concatenate([even, odd], axis=0)
    reverse = jnp.concatenate([odd, even], axis=0)
    parts = (0, 512, span)
    done = 0
    for low, high in zip(parts[:-1], parts[1:]):
        for n in range(low, high, 256):
            size = min(256, high - n)
            r_acc[:, n : n + size] = lane_contract(forward, unf[n : n + size, :]) + lane_contract(
                reverse, unf[deep + n : deep + n + size, :]
            )
        end = taps if high == span else (high - cg) // LANES * LANES
        near = slice(done, min(r_acc.shape[1], -(-(end + cg) // LANES) * LANES))
        height = near.stop - near.start
        total = r_acc[0:cg, done:end] + pltpu.roll(r_acc[cg:, near], height - cg, 1)[:, : end - done]
        if gathered:
            s_in[0, :, done:end] = total.astype(BF16)
        else:
            at = slice(done, min(s_send.shape[2], -(-end // LANES) * LANES))
            for k in range(members):
                s_send[k, :, done:end] = total[rows * k : rows * (k + 1)].astype(BF16)
            for k in range(members):
                push(
                    s_send.at[k, :, pl.ds(at.start, at.stop - at.start)],
                    s_in.at[chunk_of, :, pl.ds(at.start, at.stop - at.start)], 7, 9, group * members + k,
                )
        done = end

    for k in range(2, steps - 1):
        send_outputs(k)

    edges_arrived(cot_left, cot_right, 6, 7)
    for b in range(2):
        edge = lane_contract(
            eye[:cg, :cg],
            jnp.concatenate(
                [
                    jnp.where(has_right > 0, cot_right[8 * b : 8 * (b + 1)].astype(F32), 0.0),
                    jnp.zeros((LANES - 16, cg), F32),
                    jnp.where(has_left > 0, cot_left[8 * b : 8 * (b + 1)].astype(F32), 0.0),
                ],
                axis=0,
            ).astype(BF16),
        ).astype(BF16)
        line = jnp.concatenate(
            [cot_in[:, band * k + half * b : band * k + half * (b + 1)] for k in range(GROUPS)] + [edge], axis=1
        )
        for s in range(-2, 3):
            top = cg * (2 * (s + 2) + b)
            cot_unf[top : top + cg, :] = (line if s == 0 else pltpu.roll(line, (-s) % width, 1))[:, :q]

    def backward(i, total):
        cols = pl.ds(pl.multiple_of(i * 256, 256), 256)
        grad = dot(lhs_grad[...], cot_unf[:, cols])
        pre_grad = (grad * slope[:, cols]).astype(BF16)
        return (
            total
            + lane_contract(pre_grad[:pair], onehot[0, :, cols])
            + lane_contract(pre_grad[pair:], onehot[1, :, cols])
        )

    terms = lax.fori_loop(0, q // 256, backward, jnp.zeros((pair, 8 * SPAN), F32), unroll=True)
    shifted = jnp.concatenate([terms[cg:], jnp.zeros((cg, LANES - 8 * SPAN), F32)], axis=1)
    terms = terms[:cg, : 8 * TAPS] + pltpu.roll(shifted, LANES - 8, 1)[:, : 8 * TAPS]
    if gathered:
        t_in[0, :, : 8 * TAPS] = terms
    else:
        for k in range(members):
            t_send[k, :, : 8 * TAPS] = terms[rows * k : rows * (k + 1)]
        for k in range(members):
            push(t_send.at[k], t_in.at[chunk_of], 8, 10, group * members + k)

    send_outputs(steps - 1)

    arrived(comb_in, 8)
    for j in range(channels // band):
        part = comb_in[...].reshape(channels, band)[band * j : band * (j + 1)]
        gather = (iota((band, band), 1) == (iota((band, band), 0) % 2) * half + iota((band, band), 0) // 2)
        comb_out[:, band * j : band * (j + 1)] = lane_contract(gather.astype(F32).astype(BF16), part).astype(BF16)
    if not gathered:
        arrived(s_in, 9)
    second_out[...] = jnp.sum(s_in[:, :, :taps].astype(F32), axis=0)
    if not gathered:
        arrived(t_in, 10)
    first_out[...] = dot(split_halves(jnp.sum(t_in[:, :, : 8 * TAPS], axis=0)), diag_ref[...])

    for remote, away in started:
        if away is None:
            remote.wait_send()
            continue

        @pl.when(away)
        def _():
            remote.wait_send()


def finish_kernel(*refs):
    sems = refs[6]
    copies = [pltpu.make_async_copy(refs[k], refs[3 + k], sems.at[k]) for k in range(3)]
    for copy in copies:
        copy.start()
    for copy in copies:
        copy.wait()


def per_device(bases, base_table, first_kernel, second_kernel, cotangent):
    band, channels = cotangent.shape
    cg = channels // GROUPS
    count = lax.axis_size("seq")
    members = count // GROUPS
    rows = first_kernel.shape[0]
    gathered = rows % 16 != 0
    half = band // 2
    q = half * GROUPS
    width = q + LANES
    pair = 2 * cg
    taps = TAPS * cg
    span = SPAN * cg
    deep = 2 * (span + 64)

    lot = 1 if gathered else members
    if gathered:
        group = group_of(lax.axis_index("seq") % GROUPS)
        first_kernel, second_kernel = (
            lax.dynamic_slice_in_dim(lax.all_gather(k, "seq", axis=0, tiled=True), group * cg, cg, 0)
            for k in (first_kernel, second_kernel)
        )
        rows = cg

    vmem = pltpu.VMEM
    outs = pl.pallas_call(
        functools.partial(block_kernel, count, members, gathered),
        out_shape=(
            vmem((band, channels), BF16),
            vmem((rows, taps), F32),
            vmem((rows, taps), F32),
        ),
        in_specs=[pl.BlockSpec(memory_space=pl.ANY)] * 5,
        out_specs=[pl.BlockSpec(memory_space=vmem)] * 3,
        scratch_shapes=[
            vmem((1, band), jnp.int32),
            vmem(base_table.shape, BF16),
            vmem(first_kernel.shape, BF16),
            vmem(second_kernel.shape, BF16),
            vmem((band, channels), BF16),
            vmem((8 * TAPS, taps), BF16),
            vmem((cg, 16), BF16),
            vmem((1, band), F32),
            vmem((band, channels), BF16),
            vmem((channels, band), BF16),
            vmem((2, GROUPS, 16, cg), BF16),
            vmem((1, 2 * q), F32),
            vmem((1, band), F32),
            vmem((1, band), F32),
            vmem((rows, LANES), BF16),
            vmem((lot, rows, LANES), BF16),
            vmem((lot, rows, taps), BF16),
            vmem((cg, 2 * q), BF16),
            vmem((16, cg), BF16),
            vmem((16, cg), BF16),
            vmem((cg, 2 * q), BF16),
            vmem((GROUPS, cg, band), BF16),
            vmem((lot, rows, -(-taps // LANES) * LANES), BF16),
            vmem((lot, rows, -(-taps // LANES) * LANES), BF16),
            vmem((lot, rows, LANES), F32),
            vmem((lot, rows, LANES), F32),
            vmem((2, 8 * SPAN, width), BF16),
            vmem((2, 2 * LANES, width), BF16),
            vmem((2 * pair, q), F32),
            vmem((deep, q), BF16),
            vmem((span, q), BF16),
            vmem((pair, span + 64), F32),
            vmem((pair, deep), BF16),
            vmem((2 * pair, span), BF16),
            pltpu.SemaphoreType.DMA((9,)),
            pltpu.SemaphoreType.DMA((11,)),
            pltpu.SemaphoreType.DMA((5,)),
        ],
        compiler_params=pltpu.CompilerParams(
            collective_id=0, has_side_effects=True, vmem_limit_bytes=56 * 1024 * 1024
        ),
    )(bases.reshape(1, band), base_table, first_kernel, second_kernel, cotangent)

    outs = pl.pallas_call(
        finish_kernel,
        out_shape=tuple(jax.ShapeDtypeStruct(o.shape, o.dtype) for o in outs),
        in_specs=[pl.BlockSpec(memory_space=vmem)] * 3,
        out_specs=[pl.BlockSpec(memory_space=pl.ANY)] * 3,
        scratch_shapes=[pltpu.SemaphoreType.DMA((3,))],
    )(*[pltpu.with_memory_space_constraint(o, vmem) for o in outs])
    if gathered:
        def scatter(part):
            whole = lax.dynamic_update_slice_in_dim(jnp.zeros((channels, taps), F32), part, group * cg, 0)
            return lax.psum_scatter(whole, "seq", scatter_dimension=0, tiled=True)

        return outs[0], scatter(outs[1]), scatter(outs[2])
    return tuple(outs)


def solution(mesh):
    return jax.shard_map(
        per_device,
        mesh=mesh,
        in_specs=(
            P(("groups", "seq")),
            P(),
            P("seq", None),
            P("seq", None),
            P(("groups", "seq"), None),
        ),
        out_specs=(
            P(("groups", "seq"), None),
            P(("groups", "seq"), None),
            P(("groups", "seq"), None),
        ),
        check_vma=False,
    )
```
